32 devices in a mesh: grp: 4 (over y, core), rep: 8 (over z, x).
Axes of the slice: x: 2, y: 2, z: 4, core: 2. Of those that a mesh axis runs over, the one named last changes fastest.
Arguments:
- tokens: bfloat16 [32, 1024, 768], P(('grp', 'rep')), may hold values from -6 to 6
- segment_ids: int32 [32, 1024], P(('grp', 'rep')), may hold values from 0 to 2, as said below
- cotangent: bfloat16 [32, 1024, 768], P(('grp', 'rep')), may hold values from -6 to 6
- in_proj_master: float32 [768, 3352], P('grp'), may hold values from -0.21875 to 0.21875
- out_proj_master: float32 [1536, 768], P('grp'), may hold values from -0.15625 to 0.15625
- in_proj_error: float32 [8, 768, 3352], P('rep', 'grp'), may hold values from -6 to 6
- out_proj_error: float32 [8, 1536, 768], P('rep', 'grp'), may hold values from -6 to 6
- in_proj_moment: float32 [768, 3352], P('grp'), may hold values from -6 to 6
- out_proj_moment: float32 [1536, 768], P('grp'), may hold values from -6 to 6
- in_proj_start: float32 [4, 3352, 8], P('grp'), may hold values from -6 to 6
- out_proj_start: float32 [4, 768, 8], P('grp'), may hold values from -6 to 6
- conv_master: float32 [5, 1792], replicated, may hold values from -3 to 3
- conv_moment: float32 [5, 1792], replicated, may hold values from -6 to 6
- head_master: float32 [3, 24], replicated, may hold values from -8 to 2, as said below
- head_moment: float32 [3, 24], replicated, may hold values from -6 to 6
- norm_gain: float32 [768], replicated, may hold values from 0.5 to 1.5
- norm_gain_moment: float32 [768], replicated, may hold values from -6 to 6
- gate_gain: float32 [1536], replicated, may hold values from 0.5 to 1.5
- gate_gain_moment: float32 [1536], replicated, may hold values from -6 to 6
Outputs:
- output: bfloat16 [32, 1024, 768], P(('grp', 'rep'))
- input_grad: float32 [32, 1024, 768], P(('grp', 'rep'))
- in_proj_grad: float32 [8, 768, 3352], P('rep', 'grp')
- out_proj_grad: float32 [8, 1536, 768], P('rep', 'grp')
- in_proj_left: float32 [768, 8], P('grp')
- out_proj_left: float32 [1536, 8], P('grp')
- in_proj_right: float32 [4, 3352, 8], P('grp')
- out_proj_right: float32 [4, 768, 8], P('grp')
- in_proj_error_new: float32 [8, 768, 3352], P('rep', 'grp')
- out_proj_error_new: float32 [8, 1536, 768], P('rep', 'grp')
- in_proj_moment_new: float32 [768, 3352], P('grp')
- out_proj_moment_new: float32 [1536, 768], P('grp')
- in_proj_master_new: float32 [768, 3352], P('grp')
- out_proj_master_new: float32 [1536, 768], P('grp')
- conv_grad: float32 [5, 1792], replicated
- conv_moment_new: float32 [5, 1792], replicated
- conv_master_new: float32 [5, 1792], replicated
- head_grad: float32 [3, 24], replicated
- head_moment_new: float32 [3, 24], replicated
- head_master_new: float32 [3, 24], replicated
- norm_gain_grad: float32 [768], replicated
- norm_gain_moment_new: float32 [768], replicated
- norm_gain_new: float32 [768], replicated
- gate_gain_grad: float32 [1536], replicated
- gate_gain_moment_new: float32 [1536], replicated
- gate_gain_new: float32 [1536], replicated
The draws below stay inside these ranges and needn't reach their ends.
Inputs may be any that keep to these rules, and one draw needn't show every extreme that they name: `segment_ids`: within each sequence the ids never fall and all 3 ids occur; each document has 204 to 512 tokens and one has exactly 512. `head_master`: row 0 is the step bias, row 1 the log of the decay rate, row 2 the skip gain.
All inputs are finite; a program needn't handle non-finite values.
Results may differ from the reference program's by a relative error of at most 0.011.
Values may be sent and summed in bfloat16 or wider, within the bound.
No kernel may reach another device: no remote copies, remote signals or barrier semaphores. Data moves between devices by JAX's collectives and lax.ppermute only.
A program may use at most 256 MiB of HBM per device.

```python
import jax
import jax.numpy as jnp
from jax import lax

D = 768
HEADS = 24
HEADDIM = 64
STATE = 128
CONV = 4
SPAN = 256
RANK = 8
SEQ_DEV = 1
SEQ_LEN = 1024
INNER = 1536
CONVDIM = 1792
INPROJ = 3352
MOST = 512
LEAST = 204
SEQS = 32
N_GRP = 4
N_REP = 8


def draw_head_master(key, part):
    first, second, third = jax.random.split(key, 3)
    step_bias = jax.random.uniform(first, (HEADS,), jnp.float32, -8.0, -3.0)
    log_rate = jax.random.uniform(second, (HEADS,), jnp.float32, 0.0, 2.0)
    skip_gain = jax.random.uniform(third, (HEADS,), jnp.float32, 0.5, 1.5)
    return jnp.stack([step_bias, log_rate, skip_gain], axis=0)


def one_sequence_ids(key):
    frames = SEQ_LEN // MOST
    first, second = jax.random.split(key, 2)
    whole_frame = jax.random.randint(first, (), 0, frames)
    cuts = jax.random.randint(second, (frames,), LEAST, MOST - LEAST + 1)
    places = jnp.arange(SEQ_LEN, dtype=jnp.int32)
    frame = places // MOST
    within = places % MOST
    cut_here = jnp.sum(jnp.where(frame[:, None] == jnp.arange(frames)[None, :], cuts[None, :], 0), axis=1)
    second_doc = ((within >= cut_here) & (frame != whole_frame)).astype(jnp.int32)
    return 2 * frame - (frame > whole_frame).astype(jnp.int32) + second_doc


def draw_segment_ids(key, part):
    keys = jax.random.split(jax.random.fold_in(key, 17), SEQS)
    return jax.vmap(one_sequence_ids)(keys).astype(jnp.int32)


def block_scale(key, dims, shards, least, top_value):
    def one(position, shards_of):
        steps = jax.random.uniform(jax.random.fold_in(jax.random.fold_in(key, 6), position), (shards_of,), jnp.float32, least / len(shards), top_value / len(shards))
        return jnp.repeat(jnp.exp(steps), dims[position] // shards_of).reshape((-1,) + (1,) * (len(dims) - position - 1))

    level = one(*shards[0])
    for cut in shards[1:]:
        level = level * one(*cut)
    return level


def normal_values(rng, shape, deviation, limit, cuts=(), kind=jnp.bfloat16):
    entries = jax.random.normal(rng, shape, jnp.float32) * deviation
    if len(cuts) > 0:
        entries = block_scale(rng, shape, cuts, -0.22, 0.18) * entries
    return jnp.clip(entries, min=-limit, max=limit).astype(kind)


def setup_inputs(seed: int = 0) -> dict:
    splits = jax.random.split(jax.random.key(seed), 20)
    return {
        "tokens": normal_values(splits[0], (SEQS, SEQ_LEN, D), 1.0, 6.0, ((0, 32),)),
        "segment_ids": draw_segment_ids(jax.random.fold_in(splits[19], 71), 0),
        "cotangent": normal_values(splits[2], (SEQS, SEQ_LEN, D), 1.0, 6.0, ((0, 32),)),
        "in_proj_master": normal_values(splits[3], (D, INPROJ), D ** -0.5, 0.21875, ((0, 4),), jnp.float32),
        "out_proj_master": normal_values(splits[4], (INNER, D), INNER ** -0.5, 0.15625, ((0, 4),), jnp.float32),
        "in_proj_error": normal_values(splits[5], (N_REP, D, INPROJ), 1.0, 6.0, ((0, 8), (1, 4)), jnp.float32),
        "out_proj_error": normal_values(splits[6], (N_REP, INNER, D), 1.0, 6.0, ((0, 8), (1, 4)), jnp.float32),
        "in_proj_moment": normal_values(splits[7], (D, INPROJ), 1.0, 6.0, ((0, 4),), jnp.float32),
        "out_proj_moment": normal_values(splits[8], (INNER, D), 1.0, 6.0, ((0, 4),), jnp.float32),
        "in_proj_start": normal_values(splits[9], (N_GRP, INPROJ, RANK), 1.0, 6.0, ((0, 4),), jnp.float32),
        "out_proj_start": normal_values(splits[10], (N_GRP, D, RANK), 1.0, 6.0, ((0, 4),), jnp.float32),
        "conv_master": normal_values(splits[11], (CONV + 1, CONVDIM), CONV ** -0.5, 3.0, (), jnp.float32),
        "conv_moment": normal_values(splits[12], (CONV + 1, CONVDIM), 1.0, 6.0, (), jnp.float32),
        "head_master": draw_head_master(jax.random.fold_in(splits[19], 71), 0),
        "head_moment": normal_values(splits[14], (3, HEADS), 1.0, 6.0, (), jnp.float32),
        "norm_gain": jnp.clip(1.0 + 0.1 * jax.random.normal(splits[15], (D,), jnp.float32), 0.5, 1.5),
        "norm_gain_moment": normal_values(splits[16], (D,), 1.0, 6.0, (), jnp.float32),
        "gate_gain": jnp.clip(1.0 + 0.1 * jax.random.normal(splits[17], (INNER,), jnp.float32), 0.5, 1.5),
        "gate_gain_moment": normal_values(splits[18], (INNER,), 1.0, 6.0, (), jnp.float32),
    }


EPS = 1e-05
GS_EPS = 1e-06
MOMENTUM = 0.9
RATE = 0.01
HIGH = lax.Precision.HIGHEST

@jax.custom_vjp
def low(v):
    return lax.optimization_barrier(v.astype(jnp.bfloat16)).astype(jnp.float32)

@jax.custom_vjp
def low_back(v):
    return v

def low_keep(v):
    return (low(v), None)

def low_pass(kept, grad):
    return (grad,)

def back_keep(v):
    return (v, None)

def back_low(kept, grad):
    return (low(grad),)
low.defvjp(low_keep, low_pass)
low_back.defvjp(back_keep, back_low)

def prenorm(inputs, gain):
    return inputs * lax.rsqrt(lax.optimization_barrier(jnp.mean(inputs * inputs, axis=-1, keepdims=True)) + EPS) * gain

def conv_part(projected, conv_params, head_params, segments):
    gate_in = projected[:, :INNER]
    conv_in = projected[:, INNER:INNER + CONVDIM]
    raw_steps = projected[:, INNER + CONVDIM:]
    summed = jnp.broadcast_to(conv_params[CONV], conv_in.shape)
    for offset in range(CONV):
        tap_row = conv_params[CONV - 1 - offset]
        if offset == 0:
            summed = summed + tap_row * conv_in
        else:
            shifted = jnp.pad(conv_in[:-offset], ((offset, 0), (0, 0)))
            earlier = jnp.pad(segments[:-offset], (offset, 0), constant_values=-1)
            same_doc = (earlier == segments).astype(jnp.float32)
            summed = summed + tap_row * shifted * same_doc[:, None]
    active = jax.nn.silu(summed)
    step_sizes = jax.nn.softplus(raw_steps + head_params[0])
    return (gate_in, active, step_sizes)

def span_step(carry, block):
    state, last_doc = carry
    values, sizes, decay_log, in_b, out_c, docs = block
    cumul = jnp.cumsum(decay_log, axis=0)
    places = jnp.arange(docs.shape[0])
    allowed = (places[:, None] >= places[None, :]) & (docs[:, None] == docs[None, :])
    spread = cumul[:, None, :] - cumul[None, :, :]
    mask_three = allowed[:, :, None]
    decays = jnp.where(mask_three, jnp.exp(jnp.where(mask_three, spread, 0.0)), 0.0)
    inner_prod = jnp.dot(out_c, in_b.T, precision=HIGH)
    mixing = inner_prod[:, :, None] * decays * sizes[None, :, :]
    local_out = jnp.einsum('ijh,jhp->ihp', mixing, values, precision=HIGH)
    alive = (docs == last_doc).astype(jnp.float32)
    carried = jnp.einsum('in,hpn->ihp', out_c, state, precision=HIGH)
    carried = carried * (jnp.exp(cumul) * alive[:, None])[:, :, None]
    tail_weight = jnp.exp(cumul[-1][None, :] - cumul) * (docs == docs[-1]).astype(jnp.float32)[:, None] * sizes
    keep_rate = jnp.exp(cumul[-1]) * (docs[-1] == last_doc).astype(jnp.float32)
    added = jnp.einsum('jhp,jn->hpn', tail_weight[:, :, None] * values, in_b, precision=HIGH)
    new_state = state * keep_rate[:, None, None] + added
    return ((new_state, docs[-1]), local_out + carried)

def spanned_scan(values, sizes, decay_log, in_b, out_c, segments):
    length = values.shape[0]
    blocks = length // SPAN
    pieces = (values.reshape(blocks, SPAN, HEADS, HEADDIM), sizes.reshape(blocks, SPAN, HEADS), decay_log.reshape(blocks, SPAN, HEADS), in_b.reshape(blocks, SPAN, STATE), out_c.reshape(blocks, SPAN, STATE), segments.reshape(blocks, SPAN))
    start = (jnp.zeros((HEADS, HEADDIM, STATE), jnp.float32), jnp.array(-1, jnp.int32))
    ended, outputs = lax.scan(jax.checkpoint(span_step), start, pieces)
    return outputs.reshape(length, HEADS, HEADDIM)

def mixer_part(active, step_sizes, gate_in, head_params, gate_gain, segments):
    length = active.shape[0]
    values = active[:, :INNER].reshape(length, HEADS, HEADDIM)
    in_b = active[:, INNER:INNER + STATE]
    out_c = active[:, INNER + STATE:]
    decay_log = -step_sizes * jnp.exp(head_params[1])
    scanned = spanned_scan(values, step_sizes, decay_log, in_b, out_c, segments)
    result = (scanned + head_params[2][None, :, None] * values).reshape(length, INNER)
    gated = result * jax.nn.silu(gate_in)
    return gated * lax.rsqrt(lax.optimization_barrier(jnp.mean(gated * gated, axis=-1, keepdims=True)) + EPS) * gate_gain

def one_sequence(inputs, segments, w_in, w_out, conv_params, head_params, in_gain, gate_gain):
    normed = low(prenorm(inputs, in_gain))
    projected = low_back(jnp.dot(normed, w_in, precision=HIGH))
    gate_in, active, step_sizes = conv_part(projected, conv_params, head_params, segments)
    mixed = low(mixer_part(low(active), step_sizes, gate_in, head_params, gate_gain, segments))
    return inputs + jnp.dot(mixed, w_out, precision=HIGH)

def orthogonal(matrix):
    columns = []
    for index in range(matrix.shape[1]):
        vector = matrix[:, index]
        for done in columns:
            vector = vector - jnp.sum(done * vector) * done
        vector = vector * lax.rsqrt(jnp.sum(vector * vector) + GS_EPS)
        columns.append(vector)
    return jnp.stack(columns, axis=1)

def compress(grads, errors, starts, moment, master):
    row_count, col_count = master.shape
    rows_block = row_count // N_GRP
    whole = (grads + errors).reshape(N_REP, N_GRP, rows_block, col_count)
    lefts = jnp.einsum('rgic,gck->rgik', whole, starts, precision=HIGH)
    left_hat = jax.vmap(orthogonal)(lax.optimization_barrier(jnp.sum(lefts, axis=0)))
    rights = jnp.einsum('rgic,gik->rgck', whole, left_hat, precision=HIGH)
    right_mean = lax.optimization_barrier(jnp.sum(rights, axis=0)) / N_REP
    approx = jnp.einsum('gik,gck->gic', left_hat, right_mean, precision=HIGH)
    error_new = (whole - approx[None]).reshape(N_REP, row_count, col_count)
    approx = approx.reshape(row_count, col_count)
    moment_new = MOMENTUM * moment + approx
    master_new = master - RATE * moment_new
    return (left_hat.reshape(row_count, -1), right_mean, error_new, moment_new, master_new)

def plain_update(grad_sum, moment, master):
    moment_new = MOMENTUM * moment + grad_sum / N_REP
    return (moment_new, master - RATE * moment_new)

def reference(tokens, segment_ids, cotangent, in_proj_master, out_proj_master, in_proj_error, out_proj_error, in_proj_moment, out_proj_moment, in_proj_start, out_proj_start, conv_master, conv_moment, head_master, head_moment, norm_gain, norm_gain_moment, gate_gain, gate_gain_moment):
    w_in = lax.optimization_barrier(in_proj_master.astype(jnp.bfloat16)).astype(jnp.float32)
    w_out = lax.optimization_barrier(out_proj_master.astype(jnp.bfloat16)).astype(jnp.float32)

    def regroup(array):
        tail_shape = array.shape[1:]
        grouped = array.reshape((N_GRP, N_REP, SEQ_DEV) + tail_shape)
        return jnp.swapaxes(grouped, 0, 1).reshape((N_REP, N_GRP * SEQ_DEV) + tail_shape)

    def ungroup(array):
        tail_shape = array.shape[2:]
        grouped = array.reshape((N_REP, N_GRP, SEQ_DEV) + tail_shape)
        return jnp.swapaxes(grouped, 0, 1).reshape((SEQS,) + tail_shape)
    single = jax.checkpoint(one_sequence)

    def replica(items):
        rep_inputs, rep_segments, rep_cotangent = items

        def forward(all_inputs, win, wout, conv_params, head_params, in_gain, out_gain):

            def per_sequence(couple):
                return single(couple[0], couple[1], win, wout, conv_params, head_params, in_gain, out_gain)
            return lax.map(per_sequence, (all_inputs, rep_segments))
        outputs, backward = jax.vjp(forward, rep_inputs, w_in, w_out, conv_master, head_master, norm_gain, gate_gain)
        return (outputs,) + backward(rep_cotangent)
    results = lax.map(replica, (regroup(tokens.astype(jnp.float32)), regroup(segment_ids), regroup(cotangent.astype(jnp.float32))))
    outputs, d_inputs, g_in, g_out, g_conv, g_head, g_gain, g_gate = results
    output = ungroup(outputs).astype(jnp.bfloat16)
    input_grad = ungroup(d_inputs)
    conv_grad = lax.optimization_barrier(jnp.sum(g_conv, axis=0))
    head_grad = lax.optimization_barrier(jnp.sum(g_head, axis=0))
    norm_gain_grad = lax.optimization_barrier(jnp.sum(g_gain, axis=0))
    gate_gain_grad = lax.optimization_barrier(jnp.sum(g_gate, axis=0))
    in_left, in_right, in_err, in_mom, in_new = compress(g_in, in_proj_error, in_proj_start, in_proj_moment, in_proj_master)
    out_left, out_right, out_err, out_mom, out_new = compress(g_out, out_proj_error, out_proj_start, out_proj_moment, out_proj_master)
    conv_mom, conv_new = plain_update(conv_grad, conv_moment, conv_master)
    head_mom, head_new = plain_update(head_grad, head_moment, head_master)
    gain_mom, gain_new = plain_update(norm_gain_grad, norm_gain_moment, norm_gain)
    gate_mom, gate_new = plain_update(gate_gain_grad, gate_gain_moment, gate_gain)
    return (output, input_grad, g_in, g_out, in_left, out_left, in_right, out_right, in_err, out_err, in_mom, out_mom, in_new, out_new, conv_grad, conv_mom, conv_new, head_grad, head_mom, head_new, norm_gain_grad, gain_mom, gain_new, gate_gain_grad, gate_mom, gate_new)
```

```python
import jax
import jax.numpy as jnp
from jax import lax
from jax.experimental import pallas as pl
from jax.experimental.pallas import tpu as pltpu
from jax.sharding import PartitionSpec as P

HEADS = 24
HEADDIM = 64
STATE = 128
CONV = 4
INNER = 1536
CONVDIM = 1792
Q = 128
EPS = 1e-05
GS_EPS = 1e-06
MOMENTUM = 0.9
RATE = 0.01
LOG2E = 1.4426950408889634
F32 = jnp.float32
BF16 = jnp.bfloat16
VMEM_LIMIT = 60 * 1024 * 1024


def mm(a, b):
    return lax.dot_general(a, b, (((1,), (0,)), ((), ())), preferred_element_type=F32)


def mm_nt(a, b):
    return lax.dot_general(a, b, (((1,), (1,)), ((), ())), preferred_element_type=F32)


def split2(v):
    high = v.astype(BF16)
    return high, (v - high.astype(F32)).astype(BF16)


def split3(v):
    high = v.astype(BF16)
    rest = v - high.astype(F32)
    middle = rest.astype(BF16)
    return high, middle, (rest - middle.astype(F32)).astype(BF16)


def mm_two(a, exact):
    high, rest = split2(a)
    return mm(high, exact) + mm(rest, exact)


def mm_exact_left(exact, b):
    high, middle, rest = split3(b)
    return mm(exact, high) + mm(exact, middle) + mm(exact, rest)


def mm_three(a, b):
    a_high, a_rest = split2(a)
    b_high, b_rest = split2(b)
    return mm(a_high, b_high) + mm(a_high, b_rest) + mm(a_rest, b_high)


def sigmoid(v):
    return 0.5 * jnp.tanh(0.5 * v) + 0.5


def softplus(v):
    return jnp.maximum(v, 0.0) + jnp.log1p(jnp.exp(-jnp.abs(v)))


def whole_spec(array):
    rank = len(array.shape)
    return pl.BlockSpec(array.shape, lambda i, *_: (0,) * rank)


def row_spec(rows, cols, order=None):
    return pl.BlockSpec((rows, cols), (lambda i, *_: (i, 0)) if order is None else order)


ANY = pl.BlockSpec(memory_space=pl.ANY)
SMEM = pl.BlockSpec(memory_space=pltpu.SMEM)


def params():
    return pltpu.CompilerParams(dimension_semantics=("arbitrary",), vmem_limit_bytes=VMEM_LIMIT)


def fetch(place, pieces, buffer, sems):
    copies = []
    for index, piece in enumerate(pieces):
        copies.append(
            pltpu.make_async_copy(piece, buffer.at[jnp.bitwise_xor(place, index)], sems.at[index])
        )
    for copy in copies:
        copy.start()
    for copy in copies:
        copy.wait()


def forward_kernel(count, place, x_ref, aux_ref, segr_ref, gain_ref, conv_ref, head_ref, tri_ref, spread_ref, *rest):
    pieces = rest[:count]
    normed_ref, cin_ref, dsilu_ref, active_ref, y_ref, v_ref, cum_ref, states_ref = rest[count : count + 8]
    weights, conv_buf, state, sems = rest[count + 8 :]
    step = pl.program_id(0)

    @pl.when(step == 0)
    def _():
        fetch(place[0], pieces, weights, sems)
        conv_buf[0:8, :] = jnp.zeros((8, CONVDIM), F32)
        state[...] = jnp.zeros_like(state)

    @pl.when(step > 0)
    def _():
        conv_buf[0:8, :] = conv_buf[Q : Q + 8, :]

    x = x_ref[...].astype(F32)
    inv = lax.rsqrt(jnp.mean(x * x, axis=-1, keepdims=True) + EPS)
    normed = (x * inv * gain_ref[...]).astype(BF16)
    normed_ref[...] = normed
    weight = weights[...].reshape(weights.shape[0] * weights.shape[1], weights.shape[2])
    projected = mm(normed, weight)
    cin_ref[...] = projected[:, :CONVDIM].astype(BF16)
    conv_buf[8 : 8 + Q, :] = projected[:, :CONVDIM]
    total = conv_ref[CONV : CONV + 1, :] + conv_ref[CONV - 1 : CONV, :] * conv_buf[8 : 8 + Q, :]
    for k in range(1, CONV):
        total = total + conv_ref[CONV - 1 - k : CONV - k, :] * (conv_buf[8 - k : 8 - k + Q, :] * aux_ref[:, k : k + 1])
    gate = sigmoid(total)
    active = (total * gate).astype(BF16)
    active_ref[...] = active
    dsilu_ref[...] = (gate * (1.0 + total * (1.0 - gate))).astype(BF16)

    v = projected[:, CONVDIM : CONVDIM + HEADS] + head_ref[0:1, :HEADS]
    v_ref[...] = v
    sizes = softplus(v)
    decay_log = -sizes * jnp.exp(head_ref[1:2, :HEADS])
    cum = mm_exact_left(tri_ref[...], decay_log)
    cum_ref[...] = cum
    spread = spread_ref[...]
    alive = aux_ref[:, 7:8]
    tail = jnp.exp(cum[Q - 1 : Q, :] - cum) * aux_ref[:, 8:9] * sizes
    sizes_wide = mm_two(sizes, spread)
    alive_wide = mm_two(jnp.exp(cum) * alive, spread)
    tail_wide = mm_two(tail, spread)
    values = active[:, :INNER].astype(F32)
    in_b = active[:, INNER : INNER + STATE]
    out_c = active[:, INNER + STATE :]
    sized = (values * sizes_wide).astype(BF16)
    tailed = (values * tail_wide).astype(BF16)

    states_ref[0] = state[...].astype(BF16)
    carried = mm(out_c, state[...].astype(BF16)) * alive_wide
    state[...] = state[...] * alive_wide[Q - 1 : Q, :] + mm(in_b.astype(F32).T.astype(BF16), tailed)

    rows = lax.broadcasted_iota(jnp.int32, (Q, Q), 0)
    cols = lax.broadcasted_iota(jnp.int32, (Q, Q), 1)
    allowed = (rows >= cols) & (aux_ref[:, 0:1] == segr_ref[0])
    inner = jnp.where(allowed, mm_nt(out_c, in_b), 0.0)
    scaled = cum * LOG2E
    scaled_t = jnp.concatenate([scaled, jnp.zeros((Q, Q - HEADS), F32)], axis=1).T
    left_half = lax.broadcasted_iota(jnp.int32, (Q, 2 * HEADDIM), 1) < HEADDIM
    zero = jnp.zeros((Q, 2 * HEADDIM), BF16)
    for pair in range(HEADS // 2):
        mixes = []
        for h in (2 * pair, 2 * pair + 1):
            gap = jnp.minimum(scaled[:, h : h + 1] - scaled_t[h : h + 1, :], 0.0)
            mixes.append((inner * jnp.exp2(gap)).astype(BF16))
        block = sized[:, pair * 128 : pair * 128 + 128]
        both = jnp.concatenate([jnp.where(left_half, block, zero), jnp.where(left_half, zero, block)], axis=0)
        local = mm(jnp.concatenate(mixes, axis=1), both)
        y_ref[:, pair * 128 : pair * 128 + 128] = (local + carried[:, pair * 128 : pair * 128 + 128]).astype(BF16)


def forward_call(place, x, aux, segr, gain, conv, head, tri, spread, pieces):
    length, width = x.shape
    steps = length // Q
    count = len(pieces)
    cols = pieces[0].shape[1]
    outs = (
        jax.ShapeDtypeStruct((length, width), BF16),
        jax.ShapeDtypeStruct((length, CONVDIM), BF16),
        jax.ShapeDtypeStruct((length, CONVDIM), BF16),
        jax.ShapeDtypeStruct((length, CONVDIM), BF16),
        jax.ShapeDtypeStruct((length, INNER), BF16),
        jax.ShapeDtypeStruct((length, HEADS), F32),
        jax.ShapeDtypeStruct((length, HEADS), F32),
        jax.ShapeDtypeStruct((steps, STATE, INNER), BF16),
    )

    def kernel(*refs):
        forward_kernel(count, *refs)

    return pl.pallas_call(
        kernel,
        grid=(steps,),
        in_specs=[
            SMEM,
            row_spec(Q, width),
            row_spec(Q, aux.shape[1]),
            pl.BlockSpec((1, 1, Q), lambda i: (i, 0, 0)),
            whole_spec(gain),
            whole_spec(conv),
            whole_spec(head),
            whole_spec(tri),
            whole_spec(spread),
        ]
        + [ANY] * count,
        out_specs=[
            row_spec(Q, width),
            row_spec(Q, CONVDIM),
            row_spec(Q, CONVDIM),
            row_spec(Q, CONVDIM),
            row_spec(Q, INNER),
            row_spec(Q, HEADS),
            row_spec(Q, HEADS),
            pl.BlockSpec((1, STATE, INNER), lambda i: (i, 0, 0)),
        ],
        out_shape=outs,
        scratch_shapes=[
            pltpu.VMEM((count,) + pieces[0].shape, BF16),
            pltpu.VMEM((Q + 8, CONVDIM), F32),
            pltpu.VMEM((STATE, INNER), F32),
            pltpu.SemaphoreType.DMA((count,)),
        ],
        compiler_params=params(),
        name="forward_scan",
    )(place, x, aux, segr, gain, conv, head, tri, spread, *pieces)


def gate_kernel(count, place, normed_ref, y_ref, values_ref, x_ref, cot_ref, skip_ref, gain_ref, *rest):
    gate_pieces = rest[:count]
    out_pieces = rest[count : 2 * count]
    output_ref, mixed_ref, dgate_ref, dres_ref, sums_ref = rest[2 * count : 2 * count + 5]
    gate_w, out_w, sems = rest[2 * count + 5 :]
    step = pl.program_id(0)

    @pl.when(step == 0)
    def _():
        fetch(place[0], gate_pieces, gate_w, sems)
        fetch(place[0], out_pieces, out_w, sems)
        sums_ref[...] = jnp.zeros_like(sums_ref)

    gate_weight = gate_w[...].reshape(gate_w.shape[0] * gate_w.shape[1], gate_w.shape[2])
    out_weight = out_w[...].reshape(out_w.shape[0] * out_w.shape[1], out_w.shape[2])
    gate_in = mm(normed_ref[...], gate_weight)
    d_mixed = mm_nt(cot_ref[...], out_weight)
    gain = gain_ref[...]
    values = values_ref[...].astype(F32)
    result = y_ref[...].astype(F32) + skip_ref[...] * values
    sig = sigmoid(gate_in)
    silu = gate_in * sig
    gated = result * silu
    inv = lax.rsqrt(jnp.mean(gated * gated, axis=-1, keepdims=True) + EPS)
    unit = gated * inv
    mixed = (unit * gain).astype(BF16)
    mixed_ref[...] = mixed
    output_ref[...] = (x_ref[...].astype(F32) + mm(mixed, out_weight)).astype(BF16)
    product = d_mixed * unit
    d_unit = d_mixed * gain
    d_gated = inv * (d_unit - unit * jnp.mean(product * gain, axis=-1, keepdims=True))
    d_result = d_gated * silu
    dgate_ref[...] = (d_gated * result * (sig * (1.0 + gate_in * (1.0 - sig)))).astype(BF16)
    dres_ref[...] = d_result.astype(BF16)
    sums_ref[0:1, :] += jnp.sum(product, axis=0, keepdims=True)
    sums_ref[1:2, :] += jnp.sum(d_result * values, axis=0, keepdims=True)


def gate_call(place, normed, y, active, x, cot, skip, gain, gate_pieces, out_pieces, rows):
    length, width = x.shape
    count = len(gate_pieces)

    def kernel(*refs):
        gate_kernel(count, *refs)

    return pl.pallas_call(
        kernel,
        grid=(length // rows,),
        in_specs=[
            SMEM,
            row_spec(rows, width),
            row_spec(rows, INNER),
            row_spec(rows, INNER),
            row_spec(rows, width),
            row_spec(rows, width),
            whole_spec(skip),
            whole_spec(gain),
        ]
        + [ANY] * (2 * count),
        out_specs=[
            row_spec(rows, width),
            row_spec(rows, INNER),
            row_spec(rows, INNER),
            row_spec(rows, INNER),
            pl.BlockSpec((8, INNER), lambda i: (0, 0)),
        ],
        out_shape=(
            jax.ShapeDtypeStruct((length, width), BF16),
            jax.ShapeDtypeStruct((length, INNER), BF16),
            jax.ShapeDtypeStruct((length, INNER), BF16),
            jax.ShapeDtypeStruct((length, INNER), BF16),
            jax.ShapeDtypeStruct((8, INNER), F32),
        ),
        scratch_shapes=[
            pltpu.VMEM((count,) + gate_pieces[0].shape, BF16),
            pltpu.VMEM((count,) + out_pieces[0].shape, BF16),
            pltpu.SemaphoreType.DMA((count,)),
        ],
        compiler_params=params(),
        name="gate_both_ways",
    )(place, normed, y, active, x, cot, skip, gain, *gate_pieces, *out_pieces)


def backward_kernel(
    dy_ref, active_ref, cin_ref, dsilu_ref, v_ref, cum_ref, states_ref, aux_ref, segr_ref, conv_ref, head_ref, skip_ref,
    triu_ref, spread_ref, gather_ref, dproj_ref, dconv_ref, dhead_ref, conv_buf, dstate
):
    step = pl.program_id(0)

    @pl.when(step == 0)
    def _():
        conv_buf[...] = jnp.zeros_like(conv_buf)
        dstate[...] = jnp.zeros_like(dstate)
        dconv_ref[...] = jnp.zeros_like(dconv_ref)
        dhead_ref[...] = jnp.zeros_like(dhead_ref)

    @pl.when(step > 0)
    def _():
        conv_buf[Q : Q + 8, :] = conv_buf[0:8, :]

    spread = spread_ref[...]
    gather = gather_ref[...]
    dy = dy_ref[...]
    dy_wide = dy.astype(F32)
    values = active_ref[:, :INNER].astype(F32)
    in_b = active_ref[:, INNER : INNER + STATE]
    out_c = active_ref[:, INNER + STATE :]
    v = v_ref[...]
    cum = cum_ref[...]
    sizes = softplus(v)
    rate = jnp.exp(head_ref[1:2, :HEADS])
    alive_wide = mm_two(jnp.exp(cum) * aux_ref[:, 7:8], spread)
    tail_wide = mm_two(jnp.exp(cum[Q - 1 : Q, :] - cum) * aux_ref[:, 8:9], spread)
    sizes_wide = mm_two(sizes, spread)
    sized = (values * sizes_wide).astype(BF16)
    sized_wide = sized.astype(F32)
    entry = states_ref[0]
    grad_state = dstate[...]
    grad_low = grad_state.astype(BF16)

    carried = mm(out_c, entry) * alive_wide
    dy_alive = (dy_wide * alive_wide).astype(BF16)
    d_c = mm_nt(dy_alive, entry)
    tailed = (sized_wide * tail_wide).astype(BF16)
    d_b = mm_nt(tailed, grad_low)
    d_sized_far = mm(in_b, grad_low) * tail_wide
    keep = alive_wide[Q - 1 : Q, :]
    end_part = jnp.sum(grad_state * entry.astype(F32), axis=0, keepdims=True) * keep
    end_part = end_part + jnp.sum(sized_wide * d_sized_far, axis=0, keepdims=True)
    dstate[...] = grad_state * keep + mm(out_c.astype(F32).T.astype(BF16), dy_alive)

    rows = lax.broadcasted_iota(jnp.int32, (Q, Q), 0)
    cols = lax.broadcasted_iota(jnp.int32, (Q, Q), 1)
    allowed = (cols >= rows) & (aux_ref[:, 0:1] == segr_ref[0])
    inner = jnp.where(allowed, mm_nt(in_b, out_c), 0.0)
    scaled = cum * LOG2E
    scaled_t = jnp.concatenate([scaled, jnp.zeros((Q, Q - HEADS), F32)], axis=1).T
    left_half = lax.broadcasted_iota(jnp.int32, (Q, 2 * HEADDIM), 1) < HEADDIM
    zero = jnp.zeros((Q, 2 * HEADDIM), BF16)
    d_inner = jnp.zeros((Q, Q), F32)
    row_sums = []
    near = []
    for pair in range(HEADS // 2):
        lanes = slice(pair * 128, pair * 128 + 128)
        dy_block = dy[:, lanes]
        dy_both = jnp.concatenate(
            [jnp.where(left_half, dy_block, zero), jnp.where(left_half, zero, dy_block)], axis=0
        )
        d_mix = mm_nt(sized[:, lanes], dy_both)
        mixes = []
        for side in range(2):
            h = 2 * pair + side
            gap = jnp.minimum(scaled_t[h : h + 1, :] - scaled[:, h : h + 1], 0.0)
            decay = jnp.exp2(gap)
            mix = (inner * decay).astype(BF16)
            d_one = d_mix[:, side * Q : side * Q + Q]
            d_inner = d_inner + d_one * decay
            row_sums.append(jnp.sum(d_one * mix.astype(F32), axis=0, keepdims=True))
            mixes.append(mix)
        near.append(mm(jnp.concatenate(mixes, axis=1), dy_both))
    d_sized = jnp.concatenate(near, axis=1) + d_sized_far
    d_inner = jnp.where(allowed, d_inner, 0.0)
    d_inner_low = d_inner.astype(BF16)
    d_b = d_b + mm(d_inner_low, out_c)
    d_c = d_c + mm(d_inner.T.astype(BF16), in_b)

    row_part = jnp.concatenate(row_sums + [jnp.zeros((Q - HEADS, Q), F32)], axis=0).T[:, :HEADS]
    d_cum = row_part + mm_two(dy_wide * carried - sized_wide * d_sized, gather)[:, :HEADS]
    end_sum = mm_two(jnp.broadcast_to(end_part, (8, INNER)), gather)[0:1, :HEADS]
    d_log = mm_exact_left(triu_ref[...], d_cum) + end_sum
    d_steps = mm_two(values * d_sized, gather)[:, :HEADS] - rate * d_log
    d_v = d_steps * sigmoid(v)
    dhead_ref[0:1, :HEADS] += jnp.sum(d_v, axis=0, keepdims=True)
    dhead_ref[1:2, :HEADS] += jnp.sum(d_log * (-sizes * rate), axis=0, keepdims=True)
    dproj_ref[:, CONVDIM : CONVDIM + HEADS] = d_v.astype(BF16)

    d_values = d_sized * sizes_wide + skip_ref[...] * dy_wide
    conv_buf[0:Q, :INNER] = d_values * dsilu_ref[:, :INNER].astype(F32)
    conv_buf[0:Q, INNER : INNER + STATE] = d_b * dsilu_ref[:, INNER : INNER + STATE].astype(F32)
    conv_buf[0:Q, INNER + STATE :] = d_c * dsilu_ref[:, INNER + STATE :].astype(F32)
    cin = cin_ref[...].astype(F32)
    first = conv_buf[0:Q, :]
    total = first * conv_ref[CONV - 1 : CONV, :]
    dconv_ref[CONV : CONV + 1, :] += jnp.sum(first, axis=0, keepdims=True)
    dconv_ref[CONV - 1 : CONV, :] += jnp.sum(first * cin, axis=0, keepdims=True)
    for k in range(1, CONV):
        moved = conv_buf[k : k + Q, :] * aux_ref[:, 3 + k : 4 + k]
        total = total + moved * conv_ref[CONV - 1 - k : CONV - k, :]
        dconv_ref[CONV - 1 - k : CONV - k, :] += jnp.sum(moved * cin, axis=0, keepdims=True)
    dproj_ref[:, :CONVDIM] = total.astype(BF16)


def backward_call(dy, active, cin, dsilu, v, cum, states, aux, segr, conv, head, skip, triu, spread, gather):
    length = dy.shape[0]
    steps = length // Q

    def back(i):
        return (steps - 1 - i, 0)

    def back3(i):
        return (steps - 1 - i, 0, 0)

    return pl.pallas_call(
        backward_kernel,
        grid=(steps,),
        in_specs=[
            row_spec(Q, INNER, back),
            row_spec(Q, CONVDIM, back),
            row_spec(Q, CONVDIM, back),
            row_spec(Q, CONVDIM, back),
            row_spec(Q, HEADS, back),
            row_spec(Q, HEADS, back),
            pl.BlockSpec((1, STATE, INNER), back3),
            row_spec(Q, aux.shape[1], back),
            pl.BlockSpec((1, 1, Q), back3),
            whole_spec(conv),
            whole_spec(head),
            whole_spec(skip),
            whole_spec(triu),
            whole_spec(spread),
            whole_spec(gather),
        ],
        out_specs=[
            row_spec(Q, CONVDIM + HEADS, back),
            pl.BlockSpec((8, CONVDIM), lambda i: (0, 0)),
            pl.BlockSpec((8, 128), lambda i: (0, 0)),
        ],
        out_shape=(
            jax.ShapeDtypeStruct((length, CONVDIM + HEADS), BF16),
            jax.ShapeDtypeStruct((8, CONVDIM), F32),
            jax.ShapeDtypeStruct((8, 128), F32),
        ),
        scratch_shapes=[pltpu.VMEM((Q + 8, CONVDIM), F32), pltpu.VMEM((STATE, INNER), F32)],
        compiler_params=params(),
        name="backward_scan",
    )(dy, active, cin, dsilu, v, cum, states, aux, segr, conv, head, skip, triu, spread, gather)


def input_kernel(count, place, dgate_ref, dproj_ref, x_ref, cot_ref, gain_ref, *rest):
    gate_pieces = rest[:count]
    conv_pieces = rest[count : 2 * count]
    grad_ref, sums_ref = rest[2 * count : 2 * count + 2]
    gate_w, conv_w, sems = rest[2 * count + 2 :]
    step = pl.program_id(0)

    @pl.when(step == 0)
    def _():
        fetch(place[0], gate_pieces, gate_w, sems)
        fetch(place[0], conv_pieces, conv_w, sems)
        sums_ref[...] = jnp.zeros_like(sums_ref)

    gate_weight = gate_w[...].reshape(gate_w.shape[0] * gate_w.shape[1], gate_w.shape[2])
    conv_weight = conv_w[...].reshape(conv_w.shape[0] * conv_w.shape[1], conv_w.shape[2])
    d_normed = mm_nt(dgate_ref[...], gate_weight) + mm_nt(dproj_ref[...], conv_weight)
    x = x_ref[...].astype(F32)
    inv = lax.rsqrt(jnp.mean(x * x, axis=-1, keepdims=True) + EPS)
    unit = x * inv
    product = d_normed * unit
    gain = gain_ref[...]
    sums_ref[0:1, :] += jnp.sum(product, axis=0, keepdims=True)
    grad = inv * (d_normed * gain - unit * jnp.mean(product * gain, axis=-1, keepdims=True))
    grad_ref[...] = cot_ref[...].astype(F32) + grad


def input_call(place, dgate, dproj, x, cot, gain, gate_pieces, conv_pieces, rows):
    length, width = x.shape
    count = len(gate_pieces)

    def kernel(*refs):
        input_kernel(count, *refs)

    return pl.pallas_call(
        kernel,
        grid=(length // rows,),
        in_specs=[
            SMEM,
            row_spec(rows, dgate.shape[1]),
            row_spec(rows, dproj.shape[1]),
            row_spec(rows, width),
            row_spec(rows, width),
            whole_spec(gain),
        ]
        + [ANY] * (2 * count),
        out_specs=[row_spec(rows, width), pl.BlockSpec((8, width), lambda i: (0, 0))],
        out_shape=(jax.ShapeDtypeStruct((length, width), F32), jax.ShapeDtypeStruct((8, width), F32)),
        scratch_shapes=[
            pltpu.VMEM((count,) + gate_pieces[0].shape, BF16),
            pltpu.VMEM((count,) + conv_pieces[0].shape, BF16),
            pltpu.SemaphoreType.DMA((count,)),
        ],
        compiler_params=params(),
        name="input_grad",
    )(place, dgate, dproj, x, cot, gain, *gate_pieces, *conv_pieces)


def left_kernel(
    gate_a, gate_b, conv_a, conv_b, out_a, out_b, err_in, err_out, start_in, start_out,
    grad_in, grad_out, whole_in, whole_out, left_ref
):
    gate = gate_a[...].astype(F32) + gate_b[...].astype(F32)
    conv = conv_a[...].astype(F32) + conv_b[...].astype(F32)
    out = out_a[...].astype(F32) + out_b[...].astype(F32)
    grad_in[:, :INNER] = gate
    grad_in[:, INNER:] = conv
    grad_out[...] = out
    gate = gate + err_in[:, :INNER]
    conv = conv + err_in[:, INNER:]
    out = out + err_out[...]
    whole_in[:, :INNER] = gate
    whole_in[:, INNER:] = conv
    whole_out[...] = out
    left_in = mm_three(gate, start_in[:INNER, :]) + mm_three(conv, start_in[INNER:, :])
    left_out = mm_three(out, start_out[...])
    tall = jnp.concatenate([left_in, left_out], axis=0)
    rank = tall.shape[1]
    tall = jnp.concatenate([tall, jnp.zeros((tall.shape[0], 128 - rank), F32)], axis=1)
    extra = left_ref.shape[1] - tall.shape[0]
    if extra:
        tall = jnp.concatenate([tall, jnp.zeros((extra, 128), F32)], axis=0)
    left_ref[...] = tall.T[:rank, :]


def up(value, unit):
    return -(-value // unit) * unit


def left_call(gate, conv, out, err_in, err_out, start_in, start_out):
    rows_in, cols_in = err_in.shape
    rows_out, cols_out = err_out.shape
    rank = start_in.shape[1]
    shapes = (
        jax.ShapeDtypeStruct((rows_in, cols_in), F32),
        jax.ShapeDtypeStruct((rows_out, cols_out), F32),
        jax.ShapeDtypeStruct((rows_in, cols_in), F32),
        jax.ShapeDtypeStruct((rows_out, cols_out), F32),
        jax.ShapeDtypeStruct((rank, up(rows_in + rows_out, 128)), F32),
    )
    return pl.pallas_call(
        left_kernel,
        out_shape=shapes,
        compiler_params=pltpu.CompilerParams(vmem_limit_bytes=VMEM_LIMIT),
        name="left_factors",
    )(*gate, *conv, *out, err_in, err_out, start_in, start_out)


def gram_schmidt(rows):
    count = rows.shape[0]
    places = lax.broadcasted_iota(jnp.int32, (count, 1), 0)
    for index in range(count):
        one = rows[index : index + 1, :]
        one = one * lax.rsqrt(jnp.sum(one * one, axis=1, keepdims=True) + GS_EPS)
        shares = jnp.sum(rows * one, axis=1, keepdims=True)
        rows = jnp.where(places > index, rows - shares * one, jnp.where(places == index, one, rows))
    return rows


def right_kernel(left_ref, whole_in, whole_out, hat_in, hat_out, right_ref):
    rows_in, cols_in = whole_in.shape
    rows_out, cols_out = whole_out.shape
    rank = left_ref.shape[0]
    left = left_ref[...]
    places = lax.broadcasted_iota(jnp.int32, left.shape, 1)
    both_in = gram_schmidt(jnp.where(places < rows_in, left, 0.0))
    both_out = gram_schmidt(jnp.where((places >= rows_in) & (places < rows_in + rows_out), left, 0.0))
    tall = jnp.concatenate([both_in + both_out, jnp.zeros((128 - rank, left.shape[1]), F32)], axis=0).T
    hat_in[...] = tall[:rows_in, :rank]
    hat_out[...] = tall[rows_in : rows_in + rows_out, :rank]
    right_ref[:, :cols_in] = mm_three(both_in[:, :rows_in], whole_in[...])
    out_rows = both_out[:, rows_in : rows_in + rows_out]
    right_ref[:, up(cols_in, 128) : up(cols_in, 128) + cols_out] = mm_three(out_rows, whole_out[...])


def right_call(left, whole_in, whole_out):
    rank = left.shape[0]
    width = up(whole_in.shape[1], 128) + up(whole_out.shape[1], 128)
    return pl.pallas_call(
        right_kernel,
        out_shape=(
            jax.ShapeDtypeStruct((whole_in.shape[0], rank), F32),
            jax.ShapeDtypeStruct((whole_out.shape[0], rank), F32),
            jax.ShapeDtypeStruct((rank, width), F32),
        ),
        compiler_params=pltpu.CompilerParams(vmem_limit_bytes=VMEM_LIMIT),
        name="right_factors",
    )(left, whole_in, whole_out)


def final_kernel(
    scale, right_ref, hat_in, whole_in, mom_in, mas_in, hat_out, whole_out, mom_out, mas_out,
    right_in_ref, err_in, new_mom_in, new_mas_in, right_out_ref, err_out, new_mom_out, new_mas_out
):
    cols_in = whole_in.shape[1]
    cols_out = whole_out.shape[1]
    skip = up(cols_in, 128)
    rank = right_ref.shape[0]

    @pl.when(pl.program_id(0) == 0)
    def _():
        right = right_ref[...] * scale
        tall = jnp.concatenate([right, jnp.zeros((128 - rank, right.shape[1]), F32)], axis=0).T
        right_in_ref[...] = tall[:cols_in, :rank]
        right_out_ref[...] = tall[skip : skip + cols_out, :rank]

    def one(hat, right, whole, mom, mas, err, new_mom, new_mas):
        approx = mm_three(hat[...], right)
        err[...] = whole[...] - approx
        fresh = MOMENTUM * mom[...] + approx
        new_mom[...] = fresh
        new_mas[...] = mas[...] - RATE * fresh

    one(hat_in, right_ref[:, :cols_in] * scale, whole_in, mom_in, mas_in, err_in, new_mom_in, new_mas_in)
    one(
        hat_out, right_ref[:, skip : skip + cols_out] * scale, whole_out, mom_out, mas_out, err_out, new_mom_out, new_mas_out
    )


def final_call(scale, right, hat_in, whole_in, mom_in, mas_in, hat_out, whole_out, mom_out, mas_out, blocks):
    rank = right.shape[0]

    def kernel(*refs):
        final_kernel(scale, *refs)

    def specs(rows, cols):
        return [row_spec(rows // blocks, rank)] + [row_spec(rows // blocks, cols)] * 3

    def out_specs(rows, cols):
        return [pl.BlockSpec((cols, rank), lambda i: (0, 0))] + [row_spec(rows // blocks, cols)] * 3

    def shapes(rows, cols):
        return [jax.ShapeDtypeStruct((cols, rank), F32)] + [jax.ShapeDtypeStruct((rows, cols), F32)] * 3

    size_in, size_out = whole_in.shape, whole_out.shape
    return pl.pallas_call(
        kernel,
        grid=(blocks,),
        in_specs=[whole_spec(right)] + specs(*size_in) + specs(*size_out),
        out_specs=out_specs(*size_in) + out_specs(*size_out),
        out_shape=shapes(*size_in) + shapes(*size_out),
        compiler_params=params(),
        name="final_update",
    )(right, hat_in, whole_in, mom_in, mas_in, hat_out, whole_out, mom_out, mas_out)


def flip(value, axis, bit):
    size = lax.axis_size(axis)
    return lax.ppermute(value, axis, [(i, i ^ bit) for i in range(size)])


def bits_of(axis):
    size = lax.axis_size(axis)
    assert size & (size - 1) == 0
    return [1 << k for k in range(size.bit_length() - 1)]


def gather_pieces(shard, axis):
    pieces = {0: shard}
    for bit in reversed(bits_of(axis)):
        for index in sorted(pieces):
            pieces[index | bit] = flip(pieces[index], axis, bit)
    return [pieces[index] for index in range(len(pieces))]


def scatter_pieces(whole, axis):
    size = lax.axis_size(axis)
    place = lax.axis_index(axis)
    rows = whole.shape[0] // size
    pieces = {
        index: lax.dynamic_slice_in_dim(whole, jnp.bitwise_xor(place, index) * rows, rows, 0) for index in range(size)
    }
    bits = bits_of(axis)
    for bit in bits:
        arrived = {index: flip(pieces[index | bit], axis, bit) for index in sorted(pieces) if not index & bit}
        if bit == bits[-1]:
            return pieces[0], arrived[0]
        pieces = {
            index: (pieces[index].astype(F32) + arrived[index].astype(F32)).astype(BF16) for index in arrived
        }


def sum_all(value, axis):
    for bit in bits_of(axis):
        value = value + flip(value, axis, bit)
    return value


def rows_product(left, right):
    return lax.dot_general(left, right, (((0,), (0,)), ((), ())), preferred_element_type=F32).astype(BF16)


def plain_update(grad_sum, moment, master, replicas):
    moment_new = MOMENTUM * moment + grad_sum / replicas
    return (moment_new, master - RATE * moment_new)


def position_table(ids):
    length = ids.shape[0]
    places = jnp.arange(length)
    columns = [ids.astype(F32)]
    for k in range(1, CONV):
        earlier = jnp.concatenate([jnp.full((k,), -1, ids.dtype), ids[:-k]])
        columns.append((earlier == ids).astype(F32))
    for k in range(1, CONV):
        later = jnp.concatenate([ids[k:], jnp.full((k,), -1, ids.dtype)])
        columns.append((later == ids).astype(F32))
    ends = ids.reshape(length // Q, Q)[:, -1]
    before = jnp.concatenate([jnp.full((1,), -1, ids.dtype), ends[:-1]])
    columns.append((jnp.repeat(before, Q) == ids).astype(F32))
    columns.append((jnp.repeat(ends, Q) == ids).astype(F32))
    columns.append(places.astype(F32) * 0.0)
    return jnp.stack(columns, axis=1)


def on_device(
    tokens,
    segment_ids,
    cotangent,
    in_proj_master,
    out_proj_master,
    in_proj_error,
    out_proj_error,
    in_proj_moment,
    out_proj_moment,
    in_proj_start,
    out_proj_start,
    conv_master,
    conv_moment,
    head_master,
    head_moment,
    norm_gain,
    norm_gain_moment,
    gate_gain,
    gate_gain_moment,
):
    replicas = lax.axis_size("rep")
    x = tokens[0]
    cot = cotangent[0]
    length, width = x.shape
    place = lax.axis_index("grp").astype(jnp.int32).reshape(1)
    conv_w = gather_pieces(in_proj_master[:, INNER:].astype(BF16), "grp")
    gate_w = gather_pieces(in_proj_master[:, :INNER].astype(BF16), "grp")
    out_w = gather_pieces(out_proj_master.astype(BF16), "grp")

    aux = position_table(segment_ids[0])
    segr = segment_ids[0].astype(F32).reshape(length // Q, 1, Q)
    conv = jnp.pad(conv_master, ((0, 3), (0, 0)))
    head = jnp.pad(head_master, ((0, 5), (0, 128 - HEADS)))
    skip = jnp.repeat(head_master[2], HEADDIM)[None]
    lanes = jnp.arange(INNER) // HEADDIM
    spread = (jnp.arange(HEADS)[:, None] == lanes[None, :]).astype(BF16)
    gather = (lanes[:, None] == jnp.arange(128)[None, :]).astype(BF16)
    order = jnp.arange(Q)
    tri = (order[:, None] >= order[None, :]).astype(BF16)
    triu = (order[:, None] <= order[None, :]).astype(BF16)

    normed, cin, dsilu, active, y, v, cum, states = forward_call(
        place, x, aux, segr, norm_gain[None], conv, head, tri, spread, conv_w
    )
    output, mixed, d_gate, d_result, gate_sums = gate_call(
        place, normed, y, active, x, cot, skip, gate_gain[None], gate_w, out_w, 256
    )
    out_pair = scatter_pieces(rows_product(mixed, cot), "grp")
    gate_pair = scatter_pieces(rows_product(normed, d_gate), "grp")
    d_proj, conv_sums, head_sums = backward_call(
        d_result, active, cin, dsilu, v, cum, states, aux, segr, conv, head, skip, triu, spread, gather
    )
    conv_pair = scatter_pieces(rows_product(normed, d_proj), "grp")
    input_grad, norm_sums = input_call(place, d_gate, d_proj, x, cot, norm_gain[None], gate_w, conv_w, 256)

    skip_grad = jnp.sum(gate_sums[1].reshape(HEADS, HEADDIM), axis=1)
    small = jnp.concatenate(
        [
            conv_sums[: CONV + 1].reshape(-1),
            head_sums[0, :HEADS],
            head_sums[1, :HEADS],
            skip_grad,
            norm_sums[0],
            gate_sums[0],
        ]
    )
    count = small.shape[0]
    small = jnp.pad(small, (0, up(count, 1024) - count)).reshape(-1, 128)
    small = sum_all(sum_all(small, "grp"), "rep").reshape(-1)
    sizes = [(CONV + 1) * CONVDIM, 3 * HEADS, width, INNER]
    parts = []
    begin = 0
    for size in sizes:
        parts.append(small[begin : begin + size])
        begin += size
    conv_grad = parts[0].reshape(CONV + 1, CONVDIM)
    head_grad = parts[1].reshape(3, HEADS)
    norm_gain_grad, gate_gain_grad = parts[2], parts[3]

    in_shard, out_shard, whole_in, whole_out, left = left_call(
        gate_pair, conv_pair, out_pair, in_proj_error[0], out_proj_error[0], in_proj_start[0], out_proj_start[0]
    )
    left = sum_all(left, "rep")
    hat_in, hat_out, right = right_call(left, whole_in, whole_out)
    right = sum_all(right, "rep")
    right_in, in_err, in_mom, in_new, right_out, out_err, out_mom, out_new = final_call(
        1.0 / replicas, right, hat_in, whole_in, in_proj_moment, in_proj_master,
        hat_out, whole_out, out_proj_moment, out_proj_master, 4,
    )
    conv_mom, conv_new = plain_update(conv_grad, conv_moment, conv_master, replicas)
    head_mom, head_new = plain_update(head_grad, head_moment, head_master, replicas)
    gain_mom, gain_new = plain_update(norm_gain_grad, norm_gain_moment, norm_gain, replicas)
    gate_mom, gate_new = plain_update(gate_gain_grad, gate_gain_moment, gate_gain, replicas)
    return (
        output[None],
        input_grad[None],
        in_shard[None],
        out_shard[None],
        hat_in,
        hat_out,
        right_in[None],
        right_out[None],
        in_err[None],
        out_err[None],
        in_mom,
        out_mom,
        in_new,
        out_new,
        conv_grad,
        conv_mom,
        conv_new,
        head_grad,
        head_mom,
        head_new,
        norm_gain_grad,
        gain_mom,
        gain_new,
        gate_gain_grad,
        gate_mom,
        gate_new,
    )


def solution(mesh):
    return jax.shard_map(
        on_device,
        mesh=mesh,
        in_specs=(
            P(("grp", "rep"), None, None),
            P(("grp", "rep"), None),
            P(("grp", "rep"), None, None),
            P("grp", None),
            P("grp", None),
            P("rep", "grp", None),
            P("rep", "grp", None),
            P("grp", None),
            P("grp", None),
            P("grp", None, None),
            P("grp", None, None),
            P(),
            P(),
            P(),
            P(),
            P(),
            P(),
            P(),
            P(),
        ),
        out_specs=(
            P(("grp", "rep"), None, None),
            P(("grp", "rep"), None, None),
            P("rep", "grp", None),
            P("rep", "grp", None),
            P("grp", None),
            P("grp", None),
            P("grp", None, None),
            P("grp", None, None),
            P("rep", "grp", None),
            P("rep", "grp", None),
            P("grp", None),
            P("grp", None),
            P("grp", None),
            P("grp", None),
            P(),
            P(),
            P(),
            P(),
            P(),
            P(),
            P(),
            P(),
            P(),
            P(),
            P(),
            P(),
        ),
        check_vma=False,
    )
```

```python
import jax
import jax.numpy as jnp
from jax import lax
from jax.experimental import pallas as pl
from jax.experimental.pallas import tpu as pltpu
from jax.sharding import PartitionSpec as P


HEADS = 24
HEADDIM = 64
STATE = 128
CONV = 4
INNER = 1536
CONVDIM = 1792
Q = 128
EPS = 1e-05
GS_EPS = 1e-06
MOMENTUM = 0.9
RATE = 0.01
LOG2E = 1.4426950408889634
GATE_ROW = 5
NORM_ROW = 6
HEAD_ROW = 7
F32 = jnp.float32
BF16 = jnp.bfloat16


def mm(a, b):
    return lax.dot_general(a, b, (((1,), (0,)), ((), ())), preferred_element_type=F32)


def mm_nt(a, b):
    return lax.dot_general(a, b, (((1,), (1,)), ((), ())), preferred_element_type=F32)


def split2(v):
    high = v.astype(BF16)
    return high, (v - high.astype(F32)).astype(BF16)


def split3(v):
    high = v.astype(BF16)
    rest = v - high.astype(F32)
    middle = rest.astype(BF16)
    return high, middle, (rest - middle.astype(F32)).astype(BF16)


def mm_two(a, exact):
    high, rest = split2(a)
    return mm(high, exact) + mm(rest, exact)


def mm_exact_left(exact, b):
    high, middle, rest = split3(b)
    return mm(exact, high) + mm(exact, middle) + mm(exact, rest)


def mm_nt_three(a, b):
    a_high, a_rest = split2(a)
    b_high, b_rest = split2(b)
    return mm_nt(a_high, b_high) + mm_nt(a_high, b_rest) + mm_nt(a_rest, b_high)


def mm_three(a, b):
    a_high, a_rest = split2(a)
    b_high, b_rest = split2(b)
    return mm(a_high, b_high) + mm(a_high, b_rest) + mm(a_rest, b_high)


def sigmoid(v):
    return 0.5 * jnp.tanh(0.5 * v) + 0.5


def softplus(v):
    return jnp.maximum(v, 0.0) + jnp.log1p(jnp.exp(-jnp.abs(v)))


def hbm(array):
    return pltpu.with_memory_space_constraint(array, pltpu.HBM)


def vmem(array):
    return pltpu.with_memory_space_constraint(array, pltpu.VMEM)


def whole_spec(array):
    rank = len(array.shape)
    return pl.BlockSpec(array.shape, lambda i, *_: (0,) * rank)


def row_spec(rows, cols, order=None):
    return pl.BlockSpec((rows, cols), (lambda i, *_: (i, 0)) if order is None else order)


ANY = pl.BlockSpec(memory_space=pl.ANY)
SMEM = pl.BlockSpec(memory_space=pltpu.SMEM)


def params(mib):
    return pltpu.CompilerParams(dimension_semantics=("arbitrary",), vmem_limit_bytes=mib * 1024 * 1024)


def cost(micros):
    return pl.CostEstimate(flops=int(micros * 1e9), bytes_accessed=int(micros * 3e6), transcendentals=0)


def fetch(place, pieces, buffer, sems):
    copies = []
    for index, piece in enumerate(pieces):
        copies.append(
            pltpu.make_async_copy(piece, buffer.at[jnp.bitwise_xor(place, index)], sems.at[index])
        )
    for copy in copies:
        copy.start()
    for copy in copies:
        copy.wait()


def forward_kernel(count, place, x_ref, aux_ref, segr_ref, gain_ref, conv_ref, head_ref, tri_ref, spread_ref, *rest):
    pieces = rest[:count]
    normed_ref, cin_ref, dsilu_ref, active_ref, y_ref, v_ref, cum_ref, states_ref = rest[count : count + 8]
    weights, conv_buf, state, sems = rest[count + 8 :]
    step = pl.program_id(0)

    @pl.when(step == 0)
    def _():
        fetch(place[0], pieces, weights, sems)
        conv_buf[0:8, :] = jnp.zeros((8, CONVDIM), F32)
        state[...] = jnp.zeros_like(state)

    @pl.when(step > 0)
    def _():
        conv_buf[0:8, :] = conv_buf[Q : Q + 8, :]

    x = x_ref[...].astype(F32)
    inv = lax.rsqrt(jnp.mean(x * x, axis=-1, keepdims=True) + EPS)
    normed = (x * inv * gain_ref[...]).astype(BF16)
    normed_ref[...] = normed
    weight = weights[...].reshape(weights.shape[0] * weights.shape[1], weights.shape[2])
    projected = mm(normed, weight)
    cin_ref[...] = projected[:, :CONVDIM].astype(BF16)
    conv_buf[8 : 8 + Q, :] = projected[:, :CONVDIM]
    total = conv_ref[CONV : CONV + 1, :] + conv_ref[CONV - 1 : CONV, :] * conv_buf[8 : 8 + Q, :]
    for k in range(1, CONV):
        total = total + conv_ref[CONV - 1 - k : CONV - k, :] * (conv_buf[8 - k : 8 - k + Q, :] * aux_ref[:, k : k + 1])
    gate = sigmoid(total)
    active = (total * gate).astype(BF16)
    active_ref[...] = active
    dsilu_ref[...] = (gate * (1.0 + total * (1.0 - gate))).astype(BF16)

    v = projected[:, CONVDIM : CONVDIM + HEADS] + head_ref[0:1, :HEADS]
    v_ref[...] = v
    sizes = softplus(v)
    decay_log = -sizes * jnp.exp(head_ref[1:2, :HEADS])
    cum = mm_exact_left(tri_ref[...], decay_log)
    cum_ref[...] = cum
    spread = spread_ref[...]
    alive = aux_ref[:, 7:8]
    tail = jnp.exp(cum[Q - 1 : Q, :] - cum) * aux_ref[:, 8:9] * sizes
    sizes_wide = mm_two(sizes, spread)
    alive_wide = mm_two(jnp.exp(cum) * alive, spread)
    tail_wide = mm_two(tail, spread)
    values = active[:, :INNER].astype(F32)
    in_b = active[:, INNER : INNER + STATE]
    out_c = active[:, INNER + STATE :]
    sized = (values * sizes_wide).astype(BF16)
    tailed = (values * tail_wide).astype(BF16)

    states_ref[0] = state[...].astype(BF16)
    carried = mm(out_c, state[...].astype(BF16)) * alive_wide
    state[...] = state[...] * alive_wide[Q - 1 : Q, :] + mm(in_b.astype(F32).T.astype(BF16), tailed)

    rows = lax.broadcasted_iota(jnp.int32, (Q, Q), 0)
    cols = lax.broadcasted_iota(jnp.int32, (Q, Q), 1)
    allowed = (rows >= cols) & (aux_ref[:, 0:1] == segr_ref[0])
    inner = jnp.where(allowed, mm_nt(out_c, in_b), 0.0)
    scaled = cum * LOG2E
    scaled_t = jnp.concatenate([scaled, jnp.zeros((Q, Q - HEADS), F32)], axis=1).T
    left_half = lax.broadcasted_iota(jnp.int32, (Q, 2 * HEADDIM), 1) < HEADDIM
    zero = jnp.zeros((Q, 2 * HEADDIM), BF16)
    for pair in range(HEADS // 2):
        mixes = []
        for h in (2 * pair, 2 * pair + 1):
            gap = jnp.minimum(scaled[:, h : h + 1] - scaled_t[h : h + 1, :], 0.0)
            mixes.append((inner * jnp.exp2(gap)).astype(BF16))
        block = sized[:, pair * 128 : pair * 128 + 128]
        both = jnp.concatenate([jnp.where(left_half, block, zero), jnp.where(left_half, zero, block)], axis=0)
        local = mm(jnp.concatenate(mixes, axis=1), both)
        y_ref[:, pair * 128 : pair * 128 + 128] = (local + carried[:, pair * 128 : pair * 128 + 128]).astype(BF16)


def forward_call(place, x, aux, segr, gain, conv, head, tri, spread, pieces):
    length, width = x.shape
    steps = length // Q
    count = len(pieces)
    outs = (
        pltpu.HBM((length, width), BF16),
        pltpu.HBM((length, CONVDIM), BF16),
        pltpu.HBM((length, CONVDIM), BF16),
        pltpu.HBM((length, CONVDIM), BF16),
        pltpu.HBM((length, INNER), BF16),
        pltpu.HBM((length, HEADS), F32),
        pltpu.HBM((length, HEADS), F32),
        pltpu.HBM((steps, STATE, INNER), BF16),
    )

    def kernel(*refs):
        forward_kernel(count, *refs)

    return pl.pallas_call(
        kernel,
        grid=(steps,),
        in_specs=[
            SMEM,
            row_spec(Q, width),
            row_spec(Q, aux.shape[1]),
            pl.BlockSpec((1, 1, Q), lambda i: (i, 0, 0)),
            whole_spec(gain),
            whole_spec(conv),
            whole_spec(head),
            whole_spec(tri),
            whole_spec(spread),
        ]
        + [ANY] * count,
        out_specs=[
            row_spec(Q, width),
            row_spec(Q, CONVDIM),
            row_spec(Q, CONVDIM),
            row_spec(Q, CONVDIM),
            row_spec(Q, INNER),
            row_spec(Q, HEADS),
            row_spec(Q, HEADS),
            pl.BlockSpec((1, STATE, INNER), lambda i: (i, 0, 0)),
        ],
        out_shape=outs,
        scratch_shapes=[
            pltpu.VMEM((count,) + pieces[0].shape, BF16),
            pltpu.VMEM((Q + 8, CONVDIM), F32),
            pltpu.VMEM((STATE, INNER), F32),
            pltpu.SemaphoreType.DMA((count,)),
        ],
        compiler_params=params(28),
        cost_estimate=cost(24),
        name="forward_scan",
    )(place, hbm(x), aux, segr, gain, conv, head, tri, spread, *pieces)


def gate_kernel(count, place, normed_ref, y_ref, values_ref, x_ref, cot_ref, skip_ref, gain_ref, *rest):
    gate_pieces = rest[:count]
    out_pieces = rest[count : 2 * count]
    output_ref, mixed_ref, dgate_ref, dres_ref, sums_ref = rest[2 * count : 2 * count + 5]
    gate_w, out_w, sems = rest[2 * count + 5 :]
    step = pl.program_id(0)

    @pl.when(step == 0)
    def _():
        fetch(place[0], gate_pieces, gate_w, sems)
        fetch(place[0], out_pieces, out_w, sems)
        sums_ref[...] = jnp.zeros_like(sums_ref)

    gate_weight = gate_w[...].reshape(gate_w.shape[0] * gate_w.shape[1], gate_w.shape[2])
    out_weight = out_w[...].reshape(out_w.shape[0] * out_w.shape[1], out_w.shape[2])
    gate_in = mm(normed_ref[...], gate_weight)
    d_mixed = mm_nt(cot_ref[...], out_weight)
    gain = gain_ref[...]
    values = values_ref[...].astype(F32)
    result = y_ref[...].astype(F32) + skip_ref[...] * values
    sig = sigmoid(gate_in)
    silu = gate_in * sig
    gated = result * silu
    inv = lax.rsqrt(jnp.mean(gated * gated, axis=-1, keepdims=True) + EPS)
    unit = gated * inv
    mixed = (unit * gain).astype(BF16)
    mixed_ref[...] = mixed
    output_ref[...] = (x_ref[...].astype(F32) + mm(mixed, out_weight)).astype(BF16)
    product = d_mixed * unit
    d_unit = d_mixed * gain
    d_gated = inv * (d_unit - unit * jnp.mean(product * gain, axis=-1, keepdims=True))
    d_result = d_gated * silu
    dgate_ref[...] = (d_gated * result * (sig * (1.0 + gate_in * (1.0 - sig)))).astype(BF16)
    dres_ref[...] = d_result.astype(BF16)
    sums_ref[0:1, :] += jnp.sum(product, axis=0, keepdims=True)
    sums_ref[1:2, :] += jnp.sum(d_result * values, axis=0, keepdims=True)


def gate_call(place, normed, y, active, x, cot, skip, gain, gate_pieces, out_pieces, rows):
    length, width = x.shape
    count = len(gate_pieces)

    def kernel(*refs):
        gate_kernel(count, *refs)

    return pl.pallas_call(
        kernel,
        grid=(length // rows,),
        in_specs=[
            SMEM,
            row_spec(rows, width),
            row_spec(rows, INNER),
            row_spec(rows, INNER),
            row_spec(rows, width),
            row_spec(rows, width),
            whole_spec(skip),
            whole_spec(gain),
        ]
        + [ANY] * (2 * count),
        out_specs=[
            row_spec(rows, width),
            row_spec(rows, INNER),
            row_spec(rows, INNER),
            row_spec(rows, INNER),
            pl.BlockSpec((8, INNER), lambda i: (0, 0)),
        ],
        out_shape=(
            pltpu.HBM((length, width), BF16),
            pltpu.HBM((length, INNER), BF16),
            pltpu.HBM((length, INNER), BF16),
            pltpu.HBM((length, INNER), BF16),
            jax.ShapeDtypeStruct((8, INNER), F32),
        ),
        scratch_shapes=[
            pltpu.VMEM((count,) + gate_pieces[0].shape, BF16),
            pltpu.VMEM((count,) + out_pieces[0].shape, BF16),
            pltpu.SemaphoreType.DMA((count,)),
        ],
        compiler_params=params(40),
        cost_estimate=cost(18),
        name="gate_both_ways",
    )(place, hbm(normed), hbm(y), hbm(active), hbm(x), hbm(cot), skip, gain, *gate_pieces, *out_pieces)


def backward_kernel(
    dy_ref, active_ref, cin_ref, dsilu_ref, v_ref, cum_ref, states_ref, aux_ref, segr_ref, conv_ref, head_ref, skip_ref,
    triu_ref, spread_ref, gather_ref, dproj_ref, dconv_ref, dhead_ref, conv_buf, dstate
):
    step = pl.program_id(0)

    @pl.when(step == 0)
    def _():
        conv_buf[...] = jnp.zeros_like(conv_buf)
        dstate[...] = jnp.zeros_like(dstate)
        dconv_ref[...] = jnp.zeros_like(dconv_ref)
        dhead_ref[...] = jnp.zeros_like(dhead_ref)

    @pl.when(step > 0)
    def _():
        conv_buf[Q : Q + 8, :] = conv_buf[0:8, :]

    spread = spread_ref[...]
    gather = gather_ref[...]
    dy = dy_ref[...]
    dy_wide = dy.astype(F32)
    values = active_ref[:, :INNER].astype(F32)
    in_b = active_ref[:, INNER : INNER + STATE]
    out_c = active_ref[:, INNER + STATE :]
    v = v_ref[...]
    cum = cum_ref[...]
    sizes = softplus(v)
    rate = jnp.exp(head_ref[1:2, :HEADS])
    alive_wide = mm_two(jnp.exp(cum) * aux_ref[:, 7:8], spread)
    tail_wide = mm_two(jnp.exp(cum[Q - 1 : Q, :] - cum) * aux_ref[:, 8:9], spread)
    sizes_wide = mm_two(sizes, spread)
    sized = (values * sizes_wide).astype(BF16)
    sized_wide = sized.astype(F32)
    entry = states_ref[0]
    grad_state = dstate[...]
    grad_low = grad_state.astype(BF16)

    carried = mm(out_c, entry) * alive_wide
    dy_alive = (dy_wide * alive_wide).astype(BF16)
    d_c = mm_nt(dy_alive, entry)
    tailed = (sized_wide * tail_wide).astype(BF16)
    d_b = mm_nt(tailed, grad_low)
    d_sized_far = mm(in_b, grad_low) * tail_wide
    keep = alive_wide[Q - 1 : Q, :]
    end_part = jnp.sum(grad_state * entry.astype(F32), axis=0, keepdims=True) * keep
    end_part = end_part + jnp.sum(sized_wide * d_sized_far, axis=0, keepdims=True)
    dstate[...] = grad_state * keep + mm(out_c.astype(F32).T.astype(BF16), dy_alive)

    rows = lax.broadcasted_iota(jnp.int32, (Q, Q), 0)
    cols = lax.broadcasted_iota(jnp.int32, (Q, Q), 1)
    allowed = (cols >= rows) & (aux_ref[:, 0:1] == segr_ref[0])
    inner = jnp.where(allowed, mm_nt(in_b, out_c), 0.0)
    scaled = cum * LOG2E
    scaled_t = jnp.concatenate([scaled, jnp.zeros((Q, Q - HEADS), F32)], axis=1).T
    left_half = lax.broadcasted_iota(jnp.int32, (Q, 2 * HEADDIM), 1) < HEADDIM
    zero = jnp.zeros((Q, 2 * HEADDIM), BF16)
    d_inner = jnp.zeros((Q, Q), F32)
    row_sums = []
    near = []
    for pair in range(HEADS // 2):
        lanes = slice(pair * 128, pair * 128 + 128)
        dy_block = dy[:, lanes]
        dy_both = jnp.concatenate(
            [jnp.where(left_half, dy_block, zero), jnp.where(left_half, zero, dy_block)], axis=0
        )
        d_mix = mm_nt(sized[:, lanes], dy_both)
        mixes = []
        for side in range(2):
            h = 2 * pair + side
            gap = jnp.minimum(scaled_t[h : h + 1, :] - scaled[:, h : h + 1], 0.0)
            decay = jnp.exp2(gap)
            mix = (inner * decay).astype(BF16)
            d_one = d_mix[:, side * Q : side * Q + Q]
            d_inner = d_inner + d_one * decay
            row_sums.append(jnp.sum(d_one * mix.astype(F32), axis=0, keepdims=True))
            mixes.append(mix)
        near.append(mm(jnp.concatenate(mixes, axis=1), dy_both))
    d_sized = jnp.concatenate(near, axis=1) + d_sized_far
    d_inner = jnp.where(allowed, d_inner, 0.0)
    d_inner_low = d_inner.astype(BF16)
    d_b = d_b + mm(d_inner_low, out_c)
    d_c = d_c + mm(d_inner.T.astype(BF16), in_b)

    row_part = jnp.concatenate(row_sums + [jnp.zeros((Q - HEADS, Q), F32)], axis=0).T[:, :HEADS]
    d_cum = row_part + mm_two(dy_wide * carried - sized_wide * d_sized, gather)[:, :HEADS]
    end_sum = mm_two(jnp.broadcast_to(end_part, (8, INNER)), gather)[0:1, :HEADS]
    d_log = mm_exact_left(triu_ref[...], d_cum) + end_sum
    d_steps = mm_two(values * d_sized, gather)[:, :HEADS] - rate * d_log
    d_v = d_steps * sigmoid(v)
    dhead_ref[0:1, :HEADS] += jnp.sum(d_v, axis=0, keepdims=True)
    dhead_ref[1:2, :HEADS] += jnp.sum(d_log * (-sizes * rate), axis=0, keepdims=True)
    dproj_ref[:, CONVDIM : CONVDIM + HEADS] = d_v.astype(BF16)

    d_values = d_sized * sizes_wide + skip_ref[...] * dy_wide
    conv_buf[0:Q, :INNER] = d_values * dsilu_ref[:, :INNER].astype(F32)
    conv_buf[0:Q, INNER : INNER + STATE] = d_b * dsilu_ref[:, INNER : INNER + STATE].astype(F32)
    conv_buf[0:Q, INNER + STATE :] = d_c * dsilu_ref[:, INNER + STATE :].astype(F32)
    cin = cin_ref[...].astype(F32)
    first = conv_buf[0:Q, :]
    total = first * conv_ref[CONV - 1 : CONV, :]
    dconv_ref[CONV : CONV + 1, :] += jnp.sum(first, axis=0, keepdims=True)
    dconv_ref[CONV - 1 : CONV, :] += jnp.sum(first * cin, axis=0, keepdims=True)
    for k in range(1, CONV):
        moved = conv_buf[k : k + Q, :] * aux_ref[:, 3 + k : 4 + k]
        total = total + moved * conv_ref[CONV - 1 - k : CONV - k, :]
        dconv_ref[CONV - 1 - k : CONV - k, :] += jnp.sum(moved * cin, axis=0, keepdims=True)
    dproj_ref[:, :CONVDIM] = total.astype(BF16)


def backward_call(dy, active, cin, dsilu, v, cum, states, aux, segr, conv, head, skip, triu, spread, gather):
    length = dy.shape[0]
    steps = length // Q

    def back(i):
        return (steps - 1 - i, 0)

    def back3(i):
        return (steps - 1 - i, 0, 0)

    return pl.pallas_call(
        backward_kernel,
        grid=(steps,),
        in_specs=[
            row_spec(Q, INNER, back),
            row_spec(Q, CONVDIM, back),
            row_spec(Q, CONVDIM, back),
            row_spec(Q, CONVDIM, back),
            row_spec(Q, HEADS, back),
            row_spec(Q, HEADS, back),
            pl.BlockSpec((1, STATE, INNER), back3),
            row_spec(Q, aux.shape[1], back),
            pl.BlockSpec((1, 1, Q), back3),
            whole_spec(conv),
            whole_spec(head),
            whole_spec(skip),
            whole_spec(triu),
            whole_spec(spread),
            whole_spec(gather),
        ],
        out_specs=[
            row_spec(Q, CONVDIM + HEADS, back),
            pl.BlockSpec((8, CONVDIM), lambda i: (0, 0)),
            pl.BlockSpec((8, 128), lambda i: (0, 0)),
        ],
        out_shape=(
            pltpu.HBM((length, CONVDIM + HEADS), BF16),
            jax.ShapeDtypeStruct((8, CONVDIM), F32),
            jax.ShapeDtypeStruct((8, 128), F32),
        ),
        scratch_shapes=[pltpu.VMEM((Q + 8, CONVDIM), F32), pltpu.VMEM((STATE, INNER), F32)],
        compiler_params=params(28),
        cost_estimate=cost(40),
        name="backward_scan",
    )(
        hbm(dy), hbm(active), hbm(cin), hbm(dsilu), hbm(v), hbm(cum), hbm(states), aux, segr, conv, head, skip, triu, spread, gather
    )


def input_kernel(
    count, place, dgate_ref, dproj_ref, x_ref, cot_ref, gain_ref, conv_sums, head_sums, gate_sums, gather_ref, *rest
):
    gate_pieces = rest[:count]
    conv_pieces = rest[count : 2 * count]
    grad_ref, small_ref = rest[2 * count : 2 * count + 2]
    gate_w, conv_w, sums_ref, sems = rest[2 * count + 2 :]
    step = pl.program_id(0)

    @pl.when(step == 0)
    def _():
        fetch(place[0], gate_pieces, gate_w, sems)
        fetch(place[0], conv_pieces, conv_w, sems)
        sums_ref[...] = jnp.zeros_like(sums_ref)

    gate_weight = gate_w[...].reshape(gate_w.shape[0] * gate_w.shape[1], gate_w.shape[2])
    conv_weight = conv_w[...].reshape(conv_w.shape[0] * conv_w.shape[1], conv_w.shape[2])
    d_normed = mm_nt(dgate_ref[...], gate_weight) + mm_nt(dproj_ref[...], conv_weight)
    x = x_ref[...].astype(F32)
    inv = lax.rsqrt(jnp.mean(x * x, axis=-1, keepdims=True) + EPS)
    unit = x * inv
    product = d_normed * unit
    gain = gain_ref[...]
    sums_ref[0:1, :] += jnp.sum(product, axis=0, keepdims=True)
    grad = inv * (d_normed * gain - unit * jnp.mean(product * gain, axis=-1, keepdims=True))
    grad_ref[...] = cot_ref[...].astype(F32) + grad

    @pl.when(step == pl.num_programs(0) - 1)
    def _():
        width = gain.shape[1]
        small_ref[...] = jnp.zeros_like(small_ref)
        small_ref[0 : CONV + 1, :] = conv_sums[0 : CONV + 1, :]
        small_ref[GATE_ROW : GATE_ROW + 1, :INNER] = gate_sums[0:1, :]
        small_ref[NORM_ROW : NORM_ROW + 1, :width] = sums_ref[0:1, :]
        skip = mm_two(jnp.broadcast_to(gate_sums[1:2, :], (8, INNER)), gather_ref[...])[0:1, :]
        small_ref[HEAD_ROW : HEAD_ROW + 1, 0:128] = head_sums[0:1, :]
        small_ref[HEAD_ROW : HEAD_ROW + 1, 128:256] = head_sums[1:2, :]
        small_ref[HEAD_ROW : HEAD_ROW + 1, 256:384] = skip


def input_call(place, dgate, dproj, x, cot, gain, conv_sums, head_sums, gate_sums, gather, gate_pieces, conv_pieces, rows):
    length, width = x.shape
    count = len(gate_pieces)

    def kernel(*refs):
        input_kernel(count, *refs)

    return pl.pallas_call(
        kernel,
        grid=(length // rows,),
        in_specs=[
            SMEM,
            row_spec(rows, dgate.shape[1]),
            row_spec(rows, dproj.shape[1]),
            row_spec(rows, width),
            row_spec(rows, width),
            whole_spec(gain),
            whole_spec(conv_sums),
            whole_spec(head_sums),
            whole_spec(gate_sums),
            whole_spec(gather),
        ]
        + [ANY] * (2 * count),
        out_specs=[row_spec(rows, width), pl.BlockSpec((8, CONVDIM), lambda i: (0, 0))],
        out_shape=(pltpu.HBM((length, width), F32), jax.ShapeDtypeStruct((8, CONVDIM), F32)),
        scratch_shapes=[
            pltpu.VMEM((count,) + gate_pieces[0].shape, BF16),
            pltpu.VMEM((count,) + conv_pieces[0].shape, BF16),
            pltpu.VMEM((8, width), F32),
            pltpu.SemaphoreType.DMA((count,)),
        ],
        compiler_params=params(36),
        cost_estimate=cost(14),
        name="input_grad",
    )(place, hbm(dgate), hbm(dproj), hbm(x), hbm(cot), gain, conv_sums, head_sums, gate_sums, gather, *gate_pieces, *conv_pieces)


def up(value, unit):
    return -(-value // unit) * unit


def left_kernel(
    gate_a, gate_b, conv_a, conv_b, out_a, out_b, err_in, err_out, start_in, start_out, small_ref,
    grad_in, grad_out, whole_in, whole_out, left_ref, tall
):
    step = pl.program_id(0)
    rows_in = err_in.shape[0]
    rows_out = err_out.shape[0]
    begin = rows_in * pl.num_programs(0)
    rank = start_in.shape[0]
    lead = tall.shape[0]

    @pl.when(step == 0)
    def _():
        tall[...] = jnp.zeros_like(tall)

    gate = gate_a[...].astype(F32) + gate_b[...].astype(F32)
    conv = conv_a[...].astype(F32) + conv_b[...].astype(F32)
    out = out_a[...].astype(F32) + out_b[...].astype(F32)
    grad_in[:, :INNER] = gate
    grad_in[:, INNER:] = conv
    grad_out[...] = out
    gate = gate + err_in[:, :INNER]
    conv = conv + err_in[:, INNER:]
    out = out + err_out[...]
    whole_in[:, :INNER] = gate
    whole_in[:, INNER:] = conv
    whole_out[...] = out
    left_in = mm_nt_three(gate, start_in[:, :INNER]) + mm_nt_three(conv, start_in[:, INNER:])
    tall[pl.ds(pl.multiple_of(step * rows_in, 8), rows_in), :rank] = left_in
    tall[pl.ds(pl.multiple_of(begin + step * rows_out, 8), rows_out), :rank] = mm_nt_three(out, start_out[...])

    @pl.when(step == pl.num_programs(0) - 1)
    def _():
        left_ref[:, :lead] = tall[...].T[:rank, :]
        left_ref[:, lead:] = small_ref[...]


def left_call(gate, conv, out, err_in, err_out, start_in, start_out, small, blocks):
    rows_in, cols_in = err_in.shape
    rows_out, cols_out = err_out.shape
    rank = start_in.shape[0]
    lead = up(rows_in + rows_out, 128)
    assert rank == small.shape[0]
    part_in, part_out = rows_in // blocks, rows_out // blocks

    def both(rows_a, cols_a, rows_b, cols_b):
        return [row_spec(rows_a, cols_a), row_spec(rows_b, cols_b)]

    width = lead + small.shape[1]
    return pl.pallas_call(
        left_kernel,
        grid=(blocks,),
        in_specs=[row_spec(part_in, INNER)] * 2
        + [row_spec(part_in, cols_in - INNER)] * 2
        + [row_spec(part_out, cols_out)] * 2
        + both(part_in, cols_in, part_out, cols_out)
        + [whole_spec(start_in), whole_spec(start_out), whole_spec(small)],
        out_specs=both(part_in, cols_in, part_out, cols_out) * 2 + [pl.BlockSpec((rank, width), lambda i: (0, 0))],
        out_shape=[
            pltpu.HBM((rows_in, cols_in), F32),
            pltpu.HBM((rows_out, cols_out), F32),
            pltpu.VMEM((rows_in, cols_in), F32),
            pltpu.VMEM((rows_out, cols_out), F32),
        ]
        + [jax.ShapeDtypeStruct((rank, width), F32)],
        scratch_shapes=[pltpu.VMEM((lead, 128), F32)],
        compiler_params=params(24),
        cost_estimate=cost(6),
        name="left_factors",
    )(*gate, *conv, *out, hbm(err_in), hbm(err_out), start_in, start_out, small)


def gram_schmidt(rows):
    count = rows.shape[0]
    places = lax.broadcasted_iota(jnp.int32, (count, 1), 0)
    for index in range(count):
        one = rows[index : index + 1, :]
        one = one * lax.rsqrt(jnp.sum(one * one, axis=1, keepdims=True) + GS_EPS)
        shares = jnp.sum(rows * one, axis=1, keepdims=True)
        rows = jnp.where(places > index, rows - shares * one, jnp.where(places == index, one, rows))
    return rows


def right_kernel(lead, left_a, left_b, whole_in, whole_out, hat_in, hat_out, tall_in, tall_out, right_ref, small_ref):
    rows_in, cols_in = whole_in.shape
    rows_out, cols_out = whole_out.shape
    rank = left_a.shape[0]
    left = left_a[:, :lead] + left_b[:, :lead]
    small_ref[...] = left_a[:, lead:] + left_b[:, lead:]
    places = lax.broadcasted_iota(jnp.int32, left.shape, 1)
    both_in = gram_schmidt(jnp.where(places < rows_in, left, 0.0))
    both_out = gram_schmidt(jnp.where((places >= rows_in) & (places < rows_in + rows_out), left, 0.0))
    hats = both_in + both_out
    hat_in[...] = hats[:, :rows_in]
    hat_out[...] = hats[:, rows_in : rows_in + rows_out]
    tall = jnp.concatenate([hats, jnp.zeros((128 - rank, lead), F32)], axis=0).T
    tall_in[...] = tall[:rows_in, :rank]
    tall_out[...] = tall[rows_in : rows_in + rows_out, :rank]
    right_ref[:, :cols_in] = mm_three(both_in[:, :rows_in], whole_in[...])
    out_rows = both_out[:, rows_in : rows_in + rows_out]
    right_ref[:, up(cols_in, 128) : up(cols_in, 128) + cols_out] = mm_three(out_rows, whole_out[...])


def right_call(lead, left, whole_in, whole_out):
    rank, total = left[0].shape
    width = up(whole_in.shape[1], 128) + up(whole_out.shape[1], 128)
    rows_in, rows_out = whole_in.shape[0], whole_out.shape[0]

    def kernel(*refs):
        right_kernel(lead, *refs)

    return pl.pallas_call(
        kernel,
        out_shape=(
            jax.ShapeDtypeStruct((rank, rows_in), F32),
            jax.ShapeDtypeStruct((rank, rows_out), F32),
            jax.ShapeDtypeStruct((rows_in, rank), F32),
            jax.ShapeDtypeStruct((rows_out, rank), F32),
            jax.ShapeDtypeStruct((rank, width), F32),
            jax.ShapeDtypeStruct((rank, total - lead), F32),
        ),
        compiler_params=pltpu.CompilerParams(vmem_limit_bytes=24 * 1024 * 1024),
        cost_estimate=cost(5),
        name="right_factors",
    )(*left, vmem(whole_in), vmem(whole_out))


def final_kernel(
    scale, right_a, right_b, hat_in, whole_in, mom_in, mas_in, hat_out, whole_out, mom_out, mas_out,
    right_in_ref, err_in, new_mom_in, new_mas_in, right_out_ref, err_out, new_mom_out, new_mas_out, three
):
    cols_in = whole_in.shape[1]
    cols_out = whole_out.shape[1]
    skip = up(cols_in, 128)

    @pl.when(pl.program_id(0) == 0)
    def _():
        right = (right_a[...] + right_b[...]) * scale
        right_in_ref[...] = right[:, :cols_in]
        right_out_ref[...] = right[:, skip : skip + cols_out]
        high = right.astype(BF16).astype(F32)
        three[...] = jnp.concatenate([high, right - high, high], axis=0).astype(BF16)

    def one(hat_ref, begin, whole, mom, mas, err, new_mom, new_mas):
        hat = hat_ref[...]
        high = hat.astype(BF16).astype(F32)
        left = jnp.concatenate([high, high, hat - high], axis=1).astype(BF16)
        approx = mm(left, three[:, begin : begin + whole.shape[1]])
        err[...] = whole[...] - approx
        fresh = mom[...] + approx
        new_mom[...] = fresh
        new_mas[...] = mas[...] - RATE * fresh

    one(hat_in, 0, whole_in, mom_in, mas_in, err_in, new_mom_in, new_mas_in)
    one(hat_out, skip, whole_out, mom_out, mas_out, err_out, new_mom_out, new_mas_out)


def final_call(scale, right, hat_in, whole_in, mom_in, mas_in, hat_out, whole_out, mom_out, mas_out, blocks):
    rank, width = right[0].shape

    def kernel(*refs):
        final_kernel(scale, *refs)

    def specs(rows, cols):
        return [row_spec(rows // blocks, rank)] + [row_spec(rows // blocks, cols)] * 3

    def out_specs(rows, cols):
        return [pl.BlockSpec((rank, cols), lambda i: (0, 0))] + [row_spec(rows // blocks, cols)] * 3

    def shapes(rows, cols):
        return [jax.ShapeDtypeStruct((rank, cols), F32)] + [pltpu.HBM((rows, cols), F32)] * 3

    size_in, size_out = whole_in.shape, whole_out.shape
    return pl.pallas_call(
        kernel,
        grid=(blocks,),
        in_specs=[whole_spec(right[0])] * 2 + specs(*size_in) + specs(*size_out),
        out_specs=out_specs(*size_in) + out_specs(*size_out),
        out_shape=shapes(*size_in) + shapes(*size_out),
        scratch_shapes=[pltpu.VMEM((3 * rank, width), BF16)],
        compiler_params=params(24),
        cost_estimate=cost(10),
        name="final_update",
    )(
        *right, hat_in, vmem(whole_in), vmem(mom_in), vmem(mas_in), hat_out, vmem(whole_out), vmem(mom_out), vmem(mas_out)
    )


def decay_call(arrays, blocks):
    count = len(arrays)
    specs = [row_spec(array.shape[0] // blocks, array.shape[1]) for array in arrays]

    def kernel(*refs):
        for index in range(count):
            value = refs[index][...]
            refs[count + index][...] = MOMENTUM * value if index % 2 == 0 else value

    return pl.pallas_call(
        kernel,
        grid=(blocks,),
        in_specs=specs,
        out_specs=specs,
        out_shape=[pltpu.VMEM(array.shape, F32) for array in arrays],
        compiler_params=params(12),
        cost_estimate=cost(3),
        name="states_to_vmem",
    )(*[hbm(array) for array in arrays])


def small_kernel(replicas, sums_a, sums_b, conv_mom, conv_mas, head_mom, head_mas, norm_mom, norm_mas, gate_mom, gate_mas, *outs):
    width = norm_mom.shape[1]
    sums = sums_a[...] + sums_b[...]
    head = [sums[HEAD_ROW : HEAD_ROW + 1, 128 * k : 128 * k + HEADS] for k in range(3)]
    grads = (
        sums[0 : CONV + 1, :],
        jnp.concatenate(head, axis=0),
        sums[NORM_ROW : NORM_ROW + 1, :width],
        sums[GATE_ROW : GATE_ROW + 1, :INNER],
    )
    pairs = ((conv_mom, conv_mas), (head_mom, head_mas), (norm_mom, norm_mas), (gate_mom, gate_mas))
    for index, (grad, (moment, master)) in enumerate(zip(grads, pairs)):
        fresh = MOMENTUM * moment[...] + grad / replicas
        for place, value in enumerate((grad, fresh, master[...] - RATE * fresh)):
            out = outs[3 * index + place]
            out[...] = value.reshape(out.shape)


def small_call(replicas, sums_a, sums_b, *states):
    def kernel(*refs):
        small_kernel(replicas, *refs)

    shapes = []
    for state in states[::2]:
        shapes += [jax.ShapeDtypeStruct(state.shape[1:] if state.shape[0] == 1 else state.shape, F32)] * 3
    return pl.pallas_call(
        kernel,
        out_shape=shapes,
        compiler_params=pltpu.CompilerParams(vmem_limit_bytes=8 * 1024 * 1024),
        cost_estimate=cost(2),
        name="small_update",
    )(sums_a, sums_b, *states)


def flip(value, axis, bit):
    size = lax.axis_size(axis)
    return lax.ppermute(value, axis, [(i, i ^ bit) for i in range(size)])


def bits_of(axis):
    size = lax.axis_size(axis)
    assert size & (size - 1) == 0
    return [1 << k for k in range(size.bit_length() - 1)]


def gather_pieces(shard, axis):
    pieces = {0: shard}
    for bit in reversed(bits_of(axis)):
        for index in sorted(pieces):
            pieces[index | bit] = flip(pieces[index], axis, bit)
    return [pieces[index] for index in range(len(pieces))]


def slice_pieces(whole, axis):
    size = lax.axis_size(axis)
    place = lax.axis_index(axis)
    rows = whole.shape[0] // size
    return {
        index: lax.dynamic_slice_in_dim(whole, jnp.bitwise_xor(place, index) * rows, rows, 0) for index in range(size)
    }


def halve(pieces, axis, bit):
    arrived = {index: flip(pieces[index | bit], axis, bit) for index in sorted(pieces) if not index & bit}
    return {index: (pieces[index].astype(F32) + arrived[index].astype(F32)).astype(BF16) for index in arrived}


def halve_first(whole, axis):
    pieces = slice_pieces(whole, axis)
    for bit in bits_of(axis)[:-1]:
        pieces = halve(pieces, axis, bit)
    return pieces


def halve_last(pieces, axis):
    bit = bits_of(axis)[-1]
    return pieces[0], flip(pieces[bit], axis, bit)


def sum_pair(value, axis):
    bits = bits_of(axis)
    for bit in bits[:-1]:
        value = value + flip(value, axis, bit)
    return value, flip(value, axis, bits[-1])


def rows_product(left, right):
    return lax.dot_general(left, right, (((0,), (0,)), ((), ())), preferred_element_type=F32).astype(BF16)


def position_table(ids):
    length = ids.shape[0]
    places = jnp.arange(length)
    columns = [ids.astype(F32)]
    for k in range(1, CONV):
        earlier = jnp.concatenate([jnp.full((k,), -1, ids.dtype), ids[:-k]])
        columns.append((earlier == ids).astype(F32))
    for k in range(1, CONV):
        later = jnp.concatenate([ids[k:], jnp.full((k,), -1, ids.dtype)])
        columns.append((later == ids).astype(F32))
    ends = ids.reshape(length // Q, Q)[:, -1]
    before = jnp.concatenate([jnp.full((1,), -1, ids.dtype), ends[:-1]])
    columns.append((jnp.repeat(before, Q) == ids).astype(F32))
    columns.append((jnp.repeat(ends, Q) == ids).astype(F32))
    columns.append(places.astype(F32) * 0.0)
    return jnp.stack(columns, axis=1)


def layer_step(
    tokens,
    segment_ids,
    cotangent,
    in_proj_master,
    out_proj_master,
    in_proj_error,
    out_proj_error,
    in_proj_moment,
    out_proj_moment,
    in_proj_start,
    out_proj_start,
    conv_master,
    conv_moment,
    head_master,
    head_moment,
    norm_gain,
    norm_gain_moment,
    gate_gain,
    gate_gain_moment,
):
    replicas = lax.axis_size("rep")
    x = tokens[0]
    cot = cotangent[0]
    length, _ = x.shape
    place = lax.axis_index("grp").astype(jnp.int32).reshape(1)
    conv_w = gather_pieces(in_proj_master[:, INNER:].astype(BF16), "grp")
    gate_w = gather_pieces(in_proj_master[:, :INNER].astype(BF16), "grp")
    out_w = gather_pieces(out_proj_master.astype(BF16), "grp")

    aux = position_table(segment_ids[0])
    segr = segment_ids[0].astype(F32).reshape(length // Q, 1, Q)
    conv = jnp.pad(conv_master, ((0, 3), (0, 0)))
    head = jnp.pad(head_master, ((0, 5), (0, 128 - HEADS)))
    skip = jnp.repeat(head_master[2], HEADDIM)[None]
    lanes = jnp.arange(INNER) // HEADDIM
    spread = (jnp.arange(HEADS)[:, None] == lanes[None, :]).astype(BF16)
    gather = (lanes[:, None] == jnp.arange(128)[None, :]).astype(BF16)
    order = jnp.arange(Q)
    tri = (order[:, None] >= order[None, :]).astype(BF16)
    triu = (order[:, None] <= order[None, :]).astype(BF16)

    normed, cin, dsilu, active, y, v, cum, states = forward_call(
        place, x, aux, segr, norm_gain[None], conv, head, tri, spread, conv_w
    )
    output, mixed, d_gate, d_result, gate_sums = gate_call(
        place, normed, y, active, x, cot, skip, gate_gain[None], gate_w, out_w, 256
    )
    gate_pieces = halve_first(rows_product(normed, d_gate), "grp")
    out_pieces = halve_first(rows_product(mixed, cot), "grp")
    gate_pair = halve_last(gate_pieces, "grp")
    out_pair = halve_last(out_pieces, "grp")
    d_proj, conv_sums, head_sums = backward_call(
        d_result, active, cin, dsilu, v, cum, states, aux, segr, conv, head, skip, triu, spread, gather
    )
    conv_pair = halve_last(halve_first(rows_product(normed, d_proj), "grp"), "grp")
    input_grad, small = input_call(
        place, d_gate, d_proj, x, cot, norm_gain[None], conv_sums, head_sums, gate_sums, gather, gate_w, conv_w, 512
    )
    in_shard, out_shard, whole_in, whole_out, left = left_call(
        gate_pair, conv_pair, out_pair, in_proj_error[0], out_proj_error[0], in_proj_start[0].T, out_proj_start[0].T, small, 4
    )
    lead = left.shape[1] - small.shape[1]
    left = sum_pair(left, "rep")
    hat_in, hat_out, tall_in, tall_out, right, small = right_call(lead, left, whole_in, whole_out)
    mom_in, mas_in, mom_out, mas_out = decay_call(
        (in_proj_moment, in_proj_master, out_proj_moment, out_proj_master), 4
    )
    right = sum_pair(right, "rep")
    small = sum_pair(small, "grp")
    (
        conv_grad, conv_mom, conv_new, head_grad, head_mom, head_new,
        norm_gain_grad, gain_mom, gain_new, gate_gain_grad, gate_mom, gate_new,
    ) = small_call(
        replicas, *small, conv_moment, conv_master, head_moment, head_master,
        norm_gain_moment[None], norm_gain[None], gate_gain_moment[None], gate_gain[None],
    )
    right_in, in_err, in_mom, in_new, right_out, out_err, out_mom, out_new = final_call(
        1.0 / replicas, right, tall_in, whole_in, mom_in, mas_in, tall_out, whole_out, mom_out, mas_out, 4
    )
    return (
        output[None],
        input_grad[None],
        in_shard[None],
        out_shard[None],
        hat_in.T,
        hat_out.T,
        right_in.T[None],
        right_out.T[None],
        in_err[None],
        out_err[None],
        in_mom,
        out_mom,
        in_new,
        out_new,
        conv_grad,
        conv_mom,
        conv_new,
        head_grad,
        head_mom,
        head_new,
        norm_gain_grad,
        gain_mom,
        gain_new,
        gate_gain_grad,
        gate_mom,
        gate_new,
    )


def solution(mesh):
    return jax.shard_map(
        layer_step,
        mesh=mesh,
        in_specs=(
            P(("grp", "rep"), None, None),
            P(("grp", "rep"), None),
            P(("grp", "rep"), None, None),
            P("grp", None),
            P("grp", None),
            P("rep", "grp", None),
            P("rep", "grp", None),
            P("grp", None),
            P("grp", None),
            P("grp", None, None),
            P("grp", None, None),
            P(),
            P(),
            P(),
            P(),
            P(),
            P(),
            P(),
            P(),
        ),
        out_specs=(
            P(("grp", "rep"), None, None),
            P(("grp", "rep"), None, None),
            P("rep", "grp", None),
            P("rep", "grp", None),
            P("grp", None),
            P("grp", None),
            P("grp", None, None),
            P("grp", None, None),
            P("rep", "grp", None),
            P("rep", "grp", None),
            P("grp", None),
            P("grp", None),
            P("grp", None),
            P("grp", None),
            P(),
            P(),
            P(),
            P(),
            P(),
            P(),
            P(),
            P(),
            P(),
            P(),
            P(),
            P(),
        ),
        check_vma=False,
    )
```
